256 devices in a mesh: lev: 4 (over z_hi, core), tile: 64 (over z_lo, x, y).
Axes of the slice: x: 4, y: 4, z: 8 (z_hi: 2, z_lo: 4; z = z_hi * 4 + z_lo), core: 2. Of those that a mesh axis runs over, the one named last changes fastest.
Arguments:
- adjoint_final: float32 [6, 96, 512, 128], P(None, 'lev', 'tile'), may hold values from -6 to 6
- courant_x: float32 [96, 512, 128], P('lev', 'tile'), may hold values from 0.05 to 0.45
- courant_y: float32 [96, 512, 128], P('lev', 'tile'), may hold values from 0.05 to 0.45
- sound: float32 [96], P('lev'), may hold values from 0.1 to 0.5
- phys_jac: bfloat16 [4, 576, 576], replicated, as said below
- regime: int32 [4, 512, 128], P(None, 'tile'), may hold values from 0 to 3
- obs_operator: bfloat16 [128, 6, 96], P(None, None, 'lev'), may hold values from -0.5 to 0.5
- obs_rows: bfloat16 [4, 131072, 128], P(None, 'tile'), may hold values from -6 to 6
- obs_owner: int32 [4, 131072, 1], P(None, 'tile'), may hold values from 0 to 63; in each aligned block of 2048 rows (0 to 2047, 2048 to 4095, ..., all dimensions but the last counted through in order) at most 64 rows name the same one
- obs_cell: int32 [4, 131072], P(None, 'tile'), may hold values from 0 to 1023
- obs_count: int32 [4, 64], P(None, 'tile'), may hold values from 1 to 2048, 98304 in all within a row
Outputs:
- gradient: float32 [6, 96, 512, 128], P(None, 'lev', 'tile')
The draws below stay inside these ranges and needn't reach their ends.
Inputs may be any that keep to these rules, and one draw needn't show every extreme that they name: `obs_owner`: among the rows of one device in one step, at most 64 name one owner. `phys_jac`: A square matrix per regime.
All inputs are finite; a program needn't handle non-finite values. No bound on the sum of `obs_count` on one device may be relied on, other than what follows from the above.
Results may differ from the reference program's by a relative error of at most 0.0015.
Values may be sent and summed in bfloat16 or wider, within the bound.
A program may use at most 128 MiB of HBM per device.

```python
import math
import jax
import jax.numpy as jnp
import numpy as np
from jax import lax

F = 6
OBS_VALS = 128
NREG = 4
STEPS = 4
CX = 8
NY = 128
OBS_DEV = 2048
LEVELS = 96
NX = 512
OBS_ROWS = 131072
CAP = 64
LIVE = 98304
N_TILE = 64


def draw_phys_jac(key, part):
    width = F * LEVELS
    key_diag = jax.random.fold_in(key, 11)
    key_off = jax.random.fold_in(key, 12)
    diag = -jax.random.uniform(key_diag, (NREG, width), jnp.float32, 0.1, 0.5)
    off = 0.3 * jax.random.normal(key_off, (NREG, width, width), jnp.float32) / jnp.sqrt(float(width))
    eye = jnp.eye(width, dtype=jnp.float32)
    return (off + eye[None, :, :] * diag[:, :, None]).astype(jnp.bfloat16)


def with_ends(result, key, smallest, high):
    dims = result.shape
    spot = [jax.random.randint(jax.random.fold_in(key, axis), (), 0, dims[axis]) for axis in range(len(dims))]
    result = result.at[tuple(spot)].set(smallest)
    longest = dims.index(max(dims))
    spot[longest] = (spot[longest] + 1) % dims[longest]
    return result.at[tuple(spot)].set(high)


def block_scale(key, dims, split, low, largest):
    loudness = 1.0
    for axis_at, parts in split:
        steps = jax.random.uniform(jax.random.fold_in(jax.random.fold_in(key, 6), axis_at), (parts,), jnp.float32, low / len(split), largest / len(split))
        loudness = loudness * jnp.repeat(jnp.exp(steps), dims[axis_at] // parts).reshape((-1,) + (1,) * (len(dims) - 1 - axis_at))
    return loudness


def length_profile(number_of, total, bound, lean):
    portions = [(1 << 20) // math.isqrt(grade ** lean) + 1 for grade in range(2, number_of + 1)]
    surplus, holding = total - bound - (number_of - 1), [1] * (number_of - 1)
    while surplus > 0:
        free = [i for i in range(number_of - 1) if holding[i] < bound]
        whole, remaining = sum([portions[i] for i in free]), surplus
        for i in free:
            extra = min(bound - holding[i], max(1, remaining * portions[i] // whole), surplus)
            holding[i] = holding[i] + extra
            surplus = surplus - extra
    return np.array([bound] + holding)


def ragged(rng, count, total, reach, skew):
    if count == 2:
        one = jax.random.randint(rng, (), max(1, total - reach), min(reach, total - 1) + 1)
        return jnp.stack([one, total - one])
    lengths = jnp.asarray(length_profile(count, total, reach, skew), jnp.int32)
    pairs = (count - 1) // 2
    giver, receiver = lengths[1:1 + 2 * pairs:2], lengths[2:2 + 2 * pairs:2]
    margin = jnp.minimum(giver - 1, reach - receiver)
    passed = jax.random.randint(jax.random.fold_in(rng, 1), (pairs,), 0, 1 << 20) % (margin + 1)
    lengths = lengths.at[1:1 + 2 * pairs:2].set(giver - passed).at[2:2 + 2 * pairs:2].set(receiver + passed)
    return lengths[jax.random.permutation(jax.random.fold_in(rng, 2), count)]


def shared_out(own_key, own, number, rows, number_of, top, reach, skew):
    ranking = jax.random.permutation(own_key, number_of)
    crowded, usual = shares(number_of, rows * top, reach, skew, True), shares(number_of, rows * top, reach, skew, False)
    places = jnp.arange(number_of)

    def named(sizes, rotation):
        used = int((sizes > 0).sum())
        fixed = max(1, used // 4)
        moved = fixed + (places - fixed + rotation * (used - fixed)) % max(1, number_of - fixed)
        return jnp.zeros((number_of,), jnp.int32).at[ranking[jnp.where(places < fixed, places, moved)]].set(jnp.asarray(sizes, jnp.int32))

    sizes = jnp.where(number % 4 == 0, named(crowded, number // 4), named(usual, number - number // 4 - 1))
    mixed = jax.random.permutation(jax.random.fold_in(own, 3), number_of)
    giver, sink = mixed[0:number_of // 2 * 2:2], mixed[1:number_of // 2 * 2:2]
    room = jnp.minimum(sizes[giver] - 1, reach - sizes[sink]) // 2
    room = jnp.where((giver == ranking[0]) | (sink == ranking[0]) | (sizes[sink] == 0), 0, jnp.maximum(room, 0))
    moved = jax.random.randint(jax.random.fold_in(own, 4), (number_of // 2,), 0, 1 << 20) % (room + 1)
    sizes = sizes.at[giver].add(-moved).at[sink].add(moved)
    labels = jnp.searchsorted(jnp.cumsum(sizes), jnp.arange(rows * top), side="right").astype(jnp.int32)
    table = labels.reshape(top, rows).T
    table = table[jax.random.permutation(jax.random.fold_in(own, 1), rows)]
    rotation = jax.random.randint(jax.random.fold_in(own, 2), (rows, 1), 0, top)
    return jnp.take_along_axis(table, (jnp.arange(top)[None, :] + rotation) % top, axis=1)


def shares(number_of, total, bound, skew, full):
    loads = [(1 << 20) // math.isqrt(standing ** skew) + 1 for standing in range(1, number_of + 1)]
    largest = bound if full else min(bound, max(-(-total // number_of), total * loads[0] // sum(loads)))
    least = 1 if total - largest >= number_of - 1 else 0
    holding, spare = [largest] + [least] * (number_of - 1), total - largest - least * (number_of - 1)
    while spare > 0:
        free = [i for i in range(1, number_of) if holding[i] < largest] or [i for i in range(1, number_of) if holding[i] < bound]
        whole, remaining = sum([loads[i] for i in free]), spare
        for i in free:
            addition = min(bound - holding[i], max(1, remaining * loads[i] // whole), spare)
            holding[i] = holding[i] + addition
            spare = spare - addition
    return np.array(holding)


def centred(own_key, shape, scale, bound, pieces=(), kind=jnp.bfloat16):
    entries = scale * jax.random.normal(own_key, shape, jnp.float32)
    if pieces:
        entries = entries * block_scale(own_key, shape, pieces, -0.22, 0.18)
    return jnp.clip(entries, -bound, bound).astype(kind)


def setup_inputs(seed: int = 0) -> dict:
    key_of = jax.random.split(jax.random.key(seed), 12)
    adjoint_final = centred(key_of[0], (F, LEVELS, NX, NY), 1.0, 6.0, ((1, 4), (2, 64)), jnp.float32)
    courant_x = jnp.clip(0.05 + 0.39999999 * jax.random.uniform(key_of[1], (LEVELS, NX, NY), jnp.float32) ** block_scale(key_of[1], (LEVELS, NX, NY), ((0, 4), (1, 64)), -0.2, 0.2), 0.05, 0.45)
    courant_y = jnp.clip(0.05 + 0.39999999 * jax.random.uniform(key_of[2], (LEVELS, NX, NY), jnp.float32) ** block_scale(key_of[2], (LEVELS, NX, NY), ((0, 4), (1, 64)), -0.2, 0.2), 0.05, 0.45)
    sound = jnp.clip(jnp.exp(math.log(0.5) - 1.609438 * jax.random.uniform(key_of[3], (LEVELS,), jnp.float32) ** block_scale(key_of[3], (LEVELS,), ((0, 4),), -0.2, 0.2)), 0.1, 0.5)
    phys_jac = draw_phys_jac(jax.random.fold_in(key_of[11], 71), 0)
    regime = with_ends(jax.random.randint(key_of[5], (STEPS, NX, NY), 0, NREG), jax.random.fold_in(key_of[5], 1), 0, NREG - 1).astype(jnp.int32)
    obs_operator = centred(key_of[6], (OBS_VALS, F, LEVELS), OBS_VALS ** -0.5, 0.5, ((2, 4),))
    obs_rows = centred(key_of[7], (STEPS, OBS_ROWS, OBS_VALS), 1.0, 6.0, ((1, 64),))
    obs_owner_keys = jax.random.split(jax.random.fold_in(key_of[8], 1), STEPS * OBS_ROWS // OBS_DEV)
    obs_owner_turns = jax.random.permutation(jax.random.fold_in(key_of[8], 3), STEPS * OBS_ROWS // OBS_DEV)
    obs_owner = jax.vmap(lambda own, number: shared_out(jax.random.fold_in(key_of[8], 2), own, number, OBS_DEV, N_TILE, 1, CAP, 2))(obs_owner_keys, obs_owner_turns).reshape((STEPS, OBS_ROWS, 1))
    obs_cell = with_ends(jax.random.randint(key_of[9], (STEPS, OBS_ROWS), 0, CX * NY), jax.random.fold_in(key_of[9], 1), 0, (CX * NY) - 1).astype(jnp.int32)
    obs_count = jax.vmap(lambda own: ragged(own, N_TILE, LIVE, OBS_DEV, 2))(jax.random.split(key_of[10], STEPS)).reshape((STEPS, N_TILE)).astype(jnp.int32)
    return {"adjoint_final": adjoint_final, "courant_x": courant_x, "courant_y": courant_y, "sound": sound, "phys_jac": phys_jac, "regime": regime, "obs_operator": obs_operator, "obs_rows": obs_rows, "obs_owner": obs_owner, "obs_cell": obs_cell, "obs_count": obs_count}


def east_of(z):
    return jnp.concatenate([z[..., 1:, :], jnp.zeros_like(z[..., :1, :])], axis=-2)


def west_of(z):
    return jnp.concatenate([jnp.zeros_like(z[..., :1, :]), z[..., :-1, :]], axis=-2)


def north_of(z):
    return jnp.concatenate([z[..., 1:], jnp.zeros_like(z[..., :1])], axis=-1)


def south_of(z):
    return jnp.concatenate([jnp.zeros_like(z[..., :1]), z[..., :-1]], axis=-1)


def dynamics(lam, courant_x, courant_y, half_sound):
    advect = east_of(courant_x * lam) + north_of(courant_y * lam) - (courant_x + courant_y) * lam
    press = lam[3]
    d_u = half_sound * (east_of(press) - west_of(press))
    d_v = half_sound * (north_of(press) - south_of(press))
    d_p = half_sound * (east_of(lam[0]) - west_of(lam[0]) + north_of(lam[1]) - south_of(lam[1]))
    zeros = jnp.zeros_like(press)
    sound_term = jnp.stack([d_u, d_v, zeros, d_p, zeros, zeros])
    return lam + advect + sound_term


def reference(adjoint_final, courant_x, courant_y, sound, phys_jac, regime, obs_operator, obs_rows, obs_owner, obs_cell, obs_count):
    half_sound = (0.5 * sound)[:, None, None]
    operator_flat = obs_operator.reshape(OBS_VALS, F * LEVELS)
    row_ids = jnp.arange(OBS_ROWS, dtype=jnp.int32)
    lam = adjoint_final
    for step in range(STEPS):
        lam = dynamics(lam, courant_x, courant_y, half_sound)
        column = lam.astype(jnp.bfloat16).reshape(F * LEVELS, NX * NY)
        regime_flat = regime[step].reshape(1, NX * NY)
        delta = jnp.zeros((F * LEVELS, NX * NY), jnp.float32)
        for which in range(NREG):
            term = jnp.dot(phys_jac[which].T, column, preferred_element_type=jnp.float32)
            delta = delta + jnp.where(regime_flat == which, term, 0.0)
        delta = lax.optimization_barrier(delta.astype(jnp.bfloat16))
        lam = lam + delta.astype(jnp.float32).reshape(F, LEVELS, NX, NY)
        contrib = jnp.dot(obs_rows[step], operator_flat, preferred_element_type=jnp.float32)
        live = (row_ids % OBS_DEV) < obs_count[step][row_ids // OBS_DEV]
        target = obs_owner[step, :, 0] * (CX * NY) + obs_cell[step]
        forcing = jnp.zeros((NX * NY, F * LEVELS), jnp.float32)
        forcing = forcing.at[target].add(jnp.where(live[:, None], contrib, 0.0))
        forcing = forcing.reshape(NX, NY, F, LEVELS).transpose(2, 3, 0, 1)
        lam = lam + forcing
    return lam
```

```python
import functools

import jax
import jax.numpy as jnp
from jax import lax
from jax.experimental import pallas as pl
from jax.experimental.pallas import tpu as pltpu
from jax.sharding import PartitionSpec as P

MESH = pl.DeviceIdType.MESH
BF = jnp.bfloat16
F32 = jnp.float32
NT = (((1,), (1,)), ((), ()))


def iota(shape, dim):
    return lax.broadcasted_iota(jnp.int32, shape, dim)


def owner_lev(t, d, lev, per_z):
    h = lev // 2
    c = lev % 2
    apart = jnp.abs(t // per_z - d // per_z)
    return jnp.where(apart == 3, 1 - h, h) * 2 + c


def obs_kernel(
    op_ref, own_ref, cell_ref, cnt_ref, rows_hbm, out_ref,
    rows_v, send_rows, recv_rows, send_cell, recv_cell, oh, rc, rank_s, own_s, pmat, key_s, ohs, acc, gm, gp,
    load_sem, ss_rows, rs_rows, ss_cell, rs_cell, gs_sem, gr_sem,
):
    lev = lax.axis_index("lev")
    t = lax.axis_index("tile")
    n_tile, cap, vals = send_rows.shape[1:]
    obs = rows_v.shape[1]
    c = lev % 2
    core = lev + 1 - 2 * c
    per_z = n_tile // 4

    for j in range(2):
        pltpu.make_async_copy(rows_hbm.at[c + 2 * j], rows_v.at[j], load_sem.at[j]).start()

    barrier = pltpu.get_barrier_semaphore()

    def greet(i, _):
        d = (t + i) % n_tile
        pl.semaphore_signal(
            barrier, inc=1, device_id={"lev": owner_lev(t, d, lev, per_z), "tile": d}, device_id_type=MESH
        )
        return 0

    lax.fori_loop(1, n_tile, greet, 0)
    pl.semaphore_signal(barrier, inc=1, device_id={"lev": core, "tile": t}, device_id_type=MESH)

    upper = jnp.where(iota((128, 256), 0) < iota((128, 256), 1), 1.0, 0.0)
    upper = upper.astype(BF)
    lane128 = iota((n_tile, 128), 1)
    cells = jnp.zeros((n_tile, 128), F32)
    for j in range(2):
        step = c + 2 * j
        own = own_ref[pl.ds(step, 1), :]
        live = iota((1, obs), 1) < cnt_ref[step, 0]
        own = jnp.where(live, own, -1)
        own_s[j] = own
        oh[...] = jnp.where(own == iota((n_tile, obs), 0), 1.0, 0.0).astype(BF)
        carry = jnp.zeros((n_tile, 128), F32)
        for b in range(obs // 128):
            cols = slice(b * 128, (b + 1) * 128)
            hot = oh[:, cols]
            ex = jnp.dot(hot, upper, preferred_element_type=F32)
            rank_s[j, :, cols] = jnp.sum(hot.astype(F32) * (ex[:, :128] + carry), axis=0, keepdims=True)
            carry = carry + ex[:, 128:]
        rank = jnp.where(live, rank_s[j], -1.0)
        rank_s[j] = rank
        cell = cell_ref[pl.ds(step, 1), :]
        hot = rank == iota((cap, obs), 0).astype(F32)
        rc[:cap] = jnp.where(hot, (cell >> 7).astype(F32), 0.0).astype(BF)
        rc[cap:] = jnp.where(hot, ((cell & 127) + 1).astype(F32), 0.0).astype(BF)
        both = lax.dot_general(oh[...], rc[...], NT, preferred_element_type=F32)
        key = both * 128.0 + pltpu.roll(both, 64, axis=1)
        key = jnp.where(lane128 < 64, key, 0.0)
        cells = cells + (key if j == 0 else pltpu.roll(key, 64, axis=1))
    send_cell[...] = cells
    pl.semaphore_wait(barrier, n_tile)

    def cell_copy(d):
        return pltpu.make_async_remote_copy(
            src_ref=send_cell.at[pl.ds(d, 1), :],
            dst_ref=recv_cell.at[pl.ds(t, 1), :],
            send_sem=ss_cell.at[d],
            recv_sem=rs_cell.at[t],
            device_id={"lev": owner_lev(t, d, lev, per_z), "tile": d},
            device_id_type=MESH,
        )

    def row_copy(j, d):
        return pltpu.make_async_remote_copy(
            src_ref=send_rows.at[j, d],
            dst_ref=recv_rows.at[j, t],
            send_sem=ss_rows.at[j, d],
            recv_sem=rs_rows.at[j, t],
            device_id={"lev": owner_lev(t, d, lev, per_z), "tile": d},
            device_id_type=MESH,
        )

    def arrival(buf, sem, s):
        return pltpu.make_async_remote_copy(
            src_ref=buf, dst_ref=buf, send_sem=sem, recv_sem=sem,
            device_id={"lev": owner_lev(t, s, lev, per_z), "tile": s}, device_id_type=MESH,
        )

    def send_cells(i, _):
        cell_copy((t + i) % n_tile).start()
        return 0

    lax.fori_loop(1, n_tile, send_cells, 0)
    recv_cell[pl.ds(t, 1), :] = send_cell[pl.ds(t, 1), :]

    grp = 8
    groups = n_tile // grp
    sub16 = iota((16, obs), 0).astype(F32)

    for j in range(2):
        pltpu.make_async_copy(rows_hbm.at[c + 2 * j], rows_v.at[j], load_sem.at[j]).wait()

        def pack(g, _, j=j):
            d0 = pl.multiple_of(((g + t // grp) % groups) * grp, grp)
            for i in range(grp):
                key = jnp.where(own_s[j] == d0 + i, rank_s[j], -1.0)
                key = jnp.broadcast_to(key, (16, obs)).astype(BF)
                for q in range(cap // 16):
                    hot = key == (sub16 + 16.0 * q).astype(BF)
                    pmat[i * cap + q * 16 : i * cap + (q + 1) * 16, :] = jnp.where(
                        hot, jnp.ones((), BF), jnp.zeros((), BF)
                    )
            packed = jnp.dot(pmat[...], rows_v[j], preferred_element_type=F32)
            send_rows[j, pl.ds(d0, grp)] = packed.astype(BF).reshape(grp, cap, vals)

            def send(i, _):
                d = d0 + i

                @pl.when(d != t)
                def _():
                    row_copy(j, d).start()

                return 0

            lax.fori_loop(0, grp, send, 0)
            return 0

        lax.fori_loop(0, groups, pack, 0)
        recv_rows[j, t] = send_rows[j, t]

    def cells_in(i, _):
        s = (t + n_tile - i) % n_tile
        arrival(recv_cell.at[pl.ds(s, 1), :], rs_cell.at[s], s).wait_recv()
        return 0

    lax.fori_loop(1, n_tile, cells_in, 0)
    even = recv_cell[pl.ds(0, n_tile // 2, stride=2), :]
    odd = recv_cell[pl.ds(1, n_tile // 2, stride=2), :]
    low = iota((n_tile // 2, 128), 1) < 64
    n_x = acc.shape[0] // 128
    sub16s = iota((16, grp * cap), 0).astype(F32)
    for j in range(2):
        if j == 0:
            key = jnp.where(low, even, pltpu.roll(odd, 64, axis=1))
        else:
            key = jnp.where(low, pltpu.roll(even, 64, axis=1), odd)
        key_s[j] = key.astype(jnp.int32) - 1
        acc[...] = jnp.zeros_like(acc)

        def unpack(g, _, j=j):
            s0 = pl.multiple_of(((groups - g + t // grp) % groups) * grp, grp)

            def take(i, _):
                s = s0 + i

                @pl.when(s != t)
                def _():
                    arrival(recv_rows.at[j, s], rs_rows.at[j, s], s).wait_recv()

                return 0

            lax.fori_loop(0, grp, take, 0)
            key = jnp.concatenate(
                [key_s[j, pl.ds(s0 // 2 + q, 1), :] for q in range(grp // 2)], axis=1
            )
            cx = key >> 7
            cy = (key & 127).astype(F32)
            for x in range(n_x):
                kx = jnp.broadcast_to(jnp.where(cx == x, cy, -1.0), (16, grp * cap)).astype(BF)
                for q in range(8):
                    hot = kx == (sub16s + 16.0 * q).astype(BF)
                    ohs[x * 128 + q * 16 : x * 128 + (q + 1) * 16, :] = jnp.where(
                        hot, jnp.ones((), BF), jnp.zeros((), BF)
                    )
            rows = recv_rows[j, pl.ds(s0, grp)].reshape(grp * cap, vals)
            acc[...] += jnp.dot(ohs[...], rows, preferred_element_type=F32)
            return 0

        lax.fori_loop(0, groups, unpack, 0)
        total = acc[...]
        head = total.astype(BF)
        gm[j, :, :vals] = head
        gm[j, :, vals:] = (total - head.astype(F32)).astype(BF)
        swap(gm, gp, gs_sem, gr_sem, j, core, t).start()
        put_forcing(op_ref, gm, out_ref, j, c + 2 * j)
    for j in range(2):
        swap(gm, gp, gs_sem, gr_sem, j, core, t).wait()
        put_forcing(op_ref, gp, out_ref, j, 1 - c + 2 * j)

    def drain(i, _):
        d = (t + i) % n_tile
        cell_copy(d).wait_send()
        for j in range(2):
            row_copy(j, d).wait_send()
        return 0

    lax.fori_loop(1, n_tile, drain, 0)


def swap(gm, gp, gs_sem, gr_sem, j, core, t):
    return pltpu.make_async_remote_copy(
        src_ref=gm.at[j], dst_ref=gp.at[j], send_sem=gs_sem.at[j], recv_sem=gr_sem.at[j],
        device_id={"lev": core, "tile": t}, device_id_type=MESH,
    )


def put_forcing(op_ref, g, out_ref, j, step):
    op = op_ref[...]
    for x in range(out_ref.shape[1]):
        out_ref[step, x] = lax.dot_general(
            op, g[j, x * 128 : (x + 1) * 128, :], NT, preferred_element_type=F32
        )


def forcing_of(obs_operator, obs_rows, obs_owner, obs_cell, obs_count, n_tile, cells):
    steps, obs, vals = obs_rows.shape
    cap = max(2, 2 * obs // n_tile)
    width = obs_operator.size // vals
    op = obs_operator.reshape(vals, width).T
    op = jnp.concatenate([op, op], axis=1)
    vmem = pl.BlockSpec(memory_space=pltpu.VMEM)
    dma = pltpu.SemaphoreType.DMA
    return pl.pallas_call(
        obs_kernel,
        out_shape=jax.ShapeDtypeStruct((steps, cells // 128, width, 128), F32),
        in_specs=[
            vmem, vmem, vmem, pl.BlockSpec(memory_space=pltpu.SMEM), pl.BlockSpec(memory_space=pl.ANY),
        ],
        out_specs=vmem,
        scratch_shapes=[
            pltpu.VMEM((2, obs, vals), BF),
            pltpu.VMEM((2, n_tile, cap, vals), BF),
            pltpu.VMEM((2, n_tile, cap, vals), BF),
            pltpu.VMEM((n_tile, 128), F32),
            pltpu.VMEM((n_tile, 128), F32),
            pltpu.VMEM((n_tile, obs), BF),
            pltpu.VMEM((2 * cap, obs), BF),
            pltpu.VMEM((2, 1, obs), F32),
            pltpu.VMEM((2, 1, obs), jnp.int32),
            pltpu.VMEM((8 * cap, obs), BF),
            pltpu.VMEM((2, n_tile // 2, 128), jnp.int32),
            pltpu.VMEM((cells, 8 * cap), BF),
            pltpu.VMEM((cells, vals), F32),
            pltpu.VMEM((2, cells, 2 * vals), BF),
            pltpu.VMEM((2, cells, 2 * vals), BF),
            dma((2,)), dma((2, n_tile)), dma((2, n_tile)), dma((n_tile,)), dma((n_tile,)), dma((2,)), dma((2,)),
        ],
        compiler_params=pltpu.CompilerParams(
            collective_id=0, has_side_effects=True, vmem_limit_bytes=56 * 1024 * 1024
        ),
        name="obs",
    )(op, obs_owner.reshape(steps, obs), obs_cell, obs_count, obs_rows)


def passed_along(array, axis, by):
    devices = lax.axis_size(axis)
    pairs = [(i, i + by) for i in range(devices) if 0 <= i + by < devices]
    return lax.ppermute(array, axis, pairs)


def with_halo(block, sides, width):
    for axis, dim in sides:
        count = lax.axis_size(axis)
        forward = [(i, i + 1) for i in range(count - 1)]
        backward = [(target, source) for source, target in forward]
        low = lax.ppermute(
            lax.slice_in_dim(block, block.shape[dim] - width, None, axis=dim), axis, forward
        )
        high = lax.ppermute(lax.slice_in_dim(block, 0, width, axis=dim), axis, backward)
        block = jnp.concatenate([low, block, high], axis=dim)
    return block


def on_device(
    adjoint_final,
    courant_x,
    courant_y,
    sound,
    phys_jac,
    regime,
    obs_operator,
    obs_rows,
    obs_owner,
    obs_cell,
    obs_count,
):
    fields, lev_here, cols_x, cols_y = adjoint_final.shape
    n_tile = lax.axis_size("tile")
    n_lev = lax.axis_size("lev")
    lev_index = lax.axis_index("lev")
    steps_all, obs_dev, obs_vals = obs_rows.shape
    n_cells = cols_x * cols_y
    width_here = fields * lev_here
    levels_all = lev_here * n_lev
    width_all = fields * levels_all
    regimes = phys_jac.shape[0]
    from_east = passed_along(courant_x[:, :1, :], "tile", -1)
    courant_east = jnp.concatenate([courant_x[:, 1:, :], from_east], axis=1)
    flux_sum = courant_x + courant_y
    half_sound = (0.5 * sound)[:, None, None]
    forcing = forcing_of(obs_operator, obs_rows, obs_owner, obs_cell, obs_count, n_tile, n_cells)
    forcing = forcing.reshape(steps_all, cols_x, fields, lev_here, cols_y).transpose(0, 2, 3, 1, 4)
    quarter = n_cells // n_lev
    lam = adjoint_final
    for step in range(steps_all):
        wide = with_halo(lam, (("tile", 2),), 1)
        east = wide[:, :, 2:, :]
        west = wide[:, :, :-2, :]
        flux_y = courant_y * lam
        north_flux = jnp.concatenate([flux_y[..., 1:], jnp.zeros_like(flux_y[..., :1])], axis=-1)
        advect = courant_east * east + north_flux - flux_sum * lam
        press = lam[3]
        press_n = jnp.concatenate([press[..., 1:], jnp.zeros_like(press[..., :1])], axis=-1)
        press_s = jnp.concatenate([jnp.zeros_like(press[..., :1]), press[..., :-1]], axis=-1)
        vwind = lam[1]
        vwind_n = jnp.concatenate([vwind[..., 1:], jnp.zeros_like(vwind[..., :1])], axis=-1)
        vwind_s = jnp.concatenate([jnp.zeros_like(vwind[..., :1]), vwind[..., :-1]], axis=-1)
        d_u = half_sound * (east[3] - west[3])
        d_v = half_sound * (press_n - press_s)
        d_p = half_sound * (east[0] - west[0] + vwind_n - vwind_s)
        zeros = jnp.zeros_like(press)
        lam = lam + advect + jnp.stack([d_u, d_v, zeros, d_p, zeros, zeros])
        rounded = lam.astype(jnp.bfloat16).reshape(fields, lev_here, n_cells)
        regime_flat = regime[step].reshape(n_cells)
        column = lax.all_to_all(rounded, "lev", split_axis=2, concat_axis=1, tiled=True).reshape(
            width_all, quarter
        )
        regime_here = lax.dynamic_slice_in_dim(regime_flat, lev_index * quarter, quarter, 0)[
            None, :
        ]
        delta = jnp.zeros((width_all, quarter), jnp.float32)
        for which in range(regimes):
            term = jnp.dot(phys_jac[which].T, column, preferred_element_type=jnp.float32)
            delta = delta + jnp.where(regime_here == which, term, 0.0)
        delta = delta.astype(jnp.bfloat16).reshape(fields, levels_all, quarter)
        back = lax.all_to_all(delta, "lev", split_axis=1, concat_axis=2, tiled=True)
        lam = lam + back.astype(jnp.float32).reshape(fields, lev_here, cols_x, cols_y)
        lam = lam + forcing[step]
    return lam


def solution(mesh):
    return jax.shard_map(
        on_device,
        mesh=mesh,
        in_specs=(
            P(None, "lev", "tile", None),
            P("lev", "tile", None),
            P("lev", "tile", None),
            P("lev"),
            P(),
            P(None, "tile", None),
            P(None, None, "lev"),
            P(None, "tile", None),
            P(None, "tile", None),
            P(None, "tile"),
            P(None, "tile"),
        ),
        out_specs=P(None, "lev", "tile", None),
        check_vma=False,
    )
```

```python
import jax
import jax.numpy as jnp
import numpy as np
from jax import lax
from jax.experimental import pallas as pl
from jax.experimental.pallas import tpu as pltpu
from jax.sharding import PartitionSpec as P

MESH = pl.DeviceIdType.MESH
BF = jnp.bfloat16
F32 = jnp.float32
NT = (((1,), (1,)), ((), ()))


def iota(shape, dim):
    return lax.broadcasted_iota(jnp.int32, shape, dim)


def owner_lev(t, d, lev, per_z):
    h = lev // 2
    c = lev % 2
    apart = jnp.abs(t // per_z - d // per_z)
    return jnp.where(apart == 3, 1 - h, h) * 2 + c


def obs_kernel(
    op_ref, own_ref, cell_ref, cnt_ref, rows_hbm, out_ref,
    rows_v, send_rows, recv_rows, send_cell, recv_cell, oh, rc, rank_s, own_s, pmat, key_s, ohs, acc, gm, gp,
    load_sem, ss_rows, rs_rows, ss_cell, rs_cell, gs_sem, gr_sem,
):
    lev = lax.axis_index("lev")
    t = lax.axis_index("tile")
    n_tile, cap, vals = send_rows.shape[1:]
    obs = rows_v.shape[1]
    c = lev % 2
    core = lev + 1 - 2 * c
    per_z = n_tile // 4

    for j in range(2):
        pltpu.make_async_copy(rows_hbm.at[c + 2 * j], rows_v.at[j], load_sem.at[j]).start()

    barrier = pltpu.get_barrier_semaphore()

    def greet(i, _):
        d = (t + i) % n_tile
        pl.semaphore_signal(
            barrier, inc=1, device_id={"lev": owner_lev(t, d, lev, per_z), "tile": d}, device_id_type=MESH
        )
        return 0

    lax.fori_loop(1, n_tile, greet, 0)
    pl.semaphore_signal(barrier, inc=1, device_id={"lev": core, "tile": t}, device_id_type=MESH)

    upper = jnp.where(iota((128, 256), 0) < iota((128, 256), 1), 1.0, 0.0)
    upper = upper.astype(BF)
    lane128 = iota((n_tile, 128), 1)
    cells = jnp.zeros((n_tile, 128), F32)
    for j in range(2):
        step = c + 2 * j
        own = own_ref[pl.ds(step, 1), :]
        live = iota((1, obs), 1) < cnt_ref[step, 0]
        own = jnp.where(live, own, -1)
        own_s[j] = own
        oh[...] = jnp.where(own == iota((n_tile, obs), 0), 1.0, 0.0).astype(BF)
        carry = jnp.zeros((n_tile, 128), F32)
        for b in range(obs // 128):
            cols = slice(b * 128, (b + 1) * 128)
            hot = oh[:, cols]
            ex = jnp.dot(hot, upper, preferred_element_type=F32)
            rank_s[j, :, cols] = jnp.sum(hot.astype(F32) * (ex[:, :128] + carry), axis=0, keepdims=True)
            carry = carry + ex[:, 128:]
        rank = jnp.where(live, rank_s[j], -1.0)
        rank_s[j] = rank
        cell = cell_ref[pl.ds(step, 1), :]
        hot = rank == iota((cap, obs), 0).astype(F32)
        rc[:cap] = jnp.where(hot, (cell >> 7).astype(F32), 0.0).astype(BF)
        rc[cap:] = jnp.where(hot, ((cell & 127) + 1).astype(F32), 0.0).astype(BF)
        both = lax.dot_general(oh[...], rc[...], NT, preferred_element_type=F32)
        key = both * 128.0 + pltpu.roll(both, 64, axis=1)
        key = jnp.where(lane128 < 64, key, 0.0)
        cells = cells + (key if j == 0 else pltpu.roll(key, 64, axis=1))
    send_cell[...] = cells
    pl.semaphore_wait(barrier, n_tile)

    def cell_copy(d):
        return pltpu.make_async_remote_copy(
            src_ref=send_cell.at[pl.ds(d, 1), :],
            dst_ref=recv_cell.at[pl.ds(t, 1), :],
            send_sem=ss_cell.at[d],
            recv_sem=rs_cell.at[t],
            device_id={"lev": owner_lev(t, d, lev, per_z), "tile": d},
            device_id_type=MESH,
        )

    def row_copy(j, d):
        return pltpu.make_async_remote_copy(
            src_ref=send_rows.at[j, d],
            dst_ref=recv_rows.at[j, t],
            send_sem=ss_rows.at[j, d],
            recv_sem=rs_rows.at[j, t],
            device_id={"lev": owner_lev(t, d, lev, per_z), "tile": d},
            device_id_type=MESH,
        )

    def arrival(buf, sem, s):
        return pltpu.make_async_remote_copy(
            src_ref=buf, dst_ref=buf, send_sem=sem, recv_sem=sem,
            device_id={"lev": owner_lev(t, s, lev, per_z), "tile": s}, device_id_type=MESH,
        )

    def send_cells(i, _):
        cell_copy((t + i) % n_tile).start()
        return 0

    lax.fori_loop(1, n_tile, send_cells, 0)
    recv_cell[pl.ds(t, 1), :] = send_cell[pl.ds(t, 1), :]

    grp = 8
    groups = n_tile // grp
    sub16 = iota((16, obs), 0).astype(F32)

    for j in range(2):
        pltpu.make_async_copy(rows_hbm.at[c + 2 * j], rows_v.at[j], load_sem.at[j]).wait()

        def pack(g, _, j=j):
            d0 = pl.multiple_of(((g + t // grp) % groups) * grp, grp)
            for i in range(grp):
                key = jnp.where(own_s[j] == d0 + i, rank_s[j], -1.0)
                key = jnp.broadcast_to(key, (16, obs)).astype(BF)
                for q in range(cap // 16):
                    hot = key == (sub16 + 16.0 * q).astype(BF)
                    pmat[i * cap + q * 16 : i * cap + (q + 1) * 16, :] = jnp.where(
                        hot, jnp.ones((), BF), jnp.zeros((), BF)
                    )
            packed = jnp.dot(pmat[...], rows_v[j], preferred_element_type=F32)
            send_rows[j, pl.ds(d0, grp)] = packed.astype(BF).reshape(grp, cap, vals)

            def send(i, _):
                d = d0 + i

                @pl.when(d != t)
                def _():
                    row_copy(j, d).start()

                return 0

            lax.fori_loop(0, grp, send, 0)
            return 0

        lax.fori_loop(0, groups, pack, 0)
        recv_rows[j, t] = send_rows[j, t]

    def cells_in(i, _):
        s = (t + n_tile - i) % n_tile
        arrival(recv_cell.at[pl.ds(s, 1), :], rs_cell.at[s], s).wait_recv()
        return 0

    lax.fori_loop(1, n_tile, cells_in, 0)
    even = recv_cell[pl.ds(0, n_tile // 2, stride=2), :]
    odd = recv_cell[pl.ds(1, n_tile // 2, stride=2), :]
    low = iota((n_tile // 2, 128), 1) < 64
    n_x = acc.shape[0] // 128
    sub16s = iota((16, grp * cap), 0).astype(F32)
    for j in range(2):
        if j == 0:
            key = jnp.where(low, even, pltpu.roll(odd, 64, axis=1))
        else:
            key = jnp.where(low, pltpu.roll(even, 64, axis=1), odd)
        key_s[j] = key.astype(jnp.int32) - 1
        acc[...] = jnp.zeros_like(acc)

        def unpack(g, _, j=j):
            s0 = pl.multiple_of(((groups - g + t // grp) % groups) * grp, grp)

            def take(i, _):
                s = s0 + i

                @pl.when(s != t)
                def _():
                    arrival(recv_rows.at[j, s], rs_rows.at[j, s], s).wait_recv()

                return 0

            lax.fori_loop(0, grp, take, 0)
            key = jnp.concatenate(
                [key_s[j, pl.ds(s0 // 2 + q, 1), :] for q in range(grp // 2)], axis=1
            )
            cx = key >> 7
            cy = (key & 127).astype(F32)
            for x in range(n_x):
                kx = jnp.broadcast_to(jnp.where(cx == x, cy, -1.0), (16, grp * cap)).astype(BF)
                for q in range(8):
                    hot = kx == (sub16s + 16.0 * q).astype(BF)
                    ohs[x * 128 + q * 16 : x * 128 + (q + 1) * 16, :] = jnp.where(
                        hot, jnp.ones((), BF), jnp.zeros((), BF)
                    )
            rows = recv_rows[j, pl.ds(s0, grp)].reshape(grp * cap, vals)
            acc[...] += jnp.dot(ohs[...], rows, preferred_element_type=F32)
            return 0

        lax.fori_loop(0, groups, unpack, 0)
        total = acc[...]
        head = total.astype(BF)
        gm[j, :, :vals] = head
        gm[j, :, vals:] = (total - head.astype(F32)).astype(BF)
        swap(gm, gp, gs_sem, gr_sem, j, core, t).start()
        put_forcing(op_ref, gm, out_ref, j, c + 2 * j)
    for j in range(2):
        swap(gm, gp, gs_sem, gr_sem, j, core, t).wait()
        put_forcing(op_ref, gp, out_ref, j, 1 - c + 2 * j)

    def drain(i, _):
        d = (t + i) % n_tile
        cell_copy(d).wait_send()
        for j in range(2):
            row_copy(j, d).wait_send()
        return 0

    lax.fori_loop(1, n_tile, drain, 0)


def swap(gm, gp, gs_sem, gr_sem, j, core, t):
    return pltpu.make_async_remote_copy(
        src_ref=gm.at[j], dst_ref=gp.at[j], send_sem=gs_sem.at[j], recv_sem=gr_sem.at[j],
        device_id={"lev": core, "tile": t}, device_id_type=MESH,
    )


def put_forcing(op_ref, g, out_ref, j, step):
    op = op_ref[...]
    for x in range(out_ref.shape[1]):
        out_ref[step, x] = lax.dot_general(
            op, g[j, x * 128 : (x + 1) * 128, :], NT, preferred_element_type=F32
        )


def forcing_of(obs_operator, obs_rows, obs_owner, obs_cell, obs_count, n_tile, cells):
    steps, obs, vals = obs_rows.shape
    cap = max(2, 2 * obs // n_tile)
    width = obs_operator.size // vals
    op = obs_operator.reshape(vals, width).T
    op = jnp.concatenate([op, op], axis=1)
    vmem = pl.BlockSpec(memory_space=pltpu.VMEM)
    dma = pltpu.SemaphoreType.DMA
    return pl.pallas_call(
        obs_kernel,
        out_shape=jax.ShapeDtypeStruct((steps, cells // 128, width, 128), F32),
        in_specs=[
            vmem, vmem, vmem, pl.BlockSpec(memory_space=pltpu.SMEM), pl.BlockSpec(memory_space=pl.ANY),
        ],
        out_specs=vmem,
        scratch_shapes=[
            pltpu.VMEM((2, obs, vals), BF),
            pltpu.VMEM((2, n_tile, cap, vals), BF),
            pltpu.VMEM((2, n_tile, cap, vals), BF),
            pltpu.VMEM((n_tile, 128), F32),
            pltpu.VMEM((n_tile, 128), F32),
            pltpu.VMEM((n_tile, obs), BF),
            pltpu.VMEM((2 * cap, obs), BF),
            pltpu.VMEM((2, 1, obs), F32),
            pltpu.VMEM((2, 1, obs), jnp.int32),
            pltpu.VMEM((8 * cap, obs), BF),
            pltpu.VMEM((2, n_tile // 2, 128), jnp.int32),
            pltpu.VMEM((cells, 8 * cap), BF),
            pltpu.VMEM((cells, vals), F32),
            pltpu.VMEM((2, cells, 2 * vals), BF),
            pltpu.VMEM((2, cells, 2 * vals), BF),
            dma((2,)), dma((2, n_tile)), dma((2, n_tile)), dma((n_tile,)), dma((n_tile,)), dma((2,)), dma((2,)),
        ],
        compiler_params=pltpu.CompilerParams(
            collective_id=0, has_side_effects=True, vmem_limit_bytes=56 * 1024 * 1024
        ),
        name="obs",
    )(op, obs_owner.reshape(steps, obs), obs_cell, obs_count, obs_rows)


def step_kernel(
    lam_ref, cx_ref, cy_ref, hs_ref, reg_ref, frc_hbm, jac_hbm, perm_hbm, out_ref,
    a_s, b_s, cx_s, cy_s, frc_s, jac_s, perm_s, jt_s, col, east_in, west_in, edge_out, rim_out, cxe_in,
    load_sem, zs, zr, ks, kr, fs, fr, es, er, ws, wr, cs, cr,
):
    lev = lax.axis_index("lev")
    t = lax.axis_index("tile")
    n_tile = lax.axis_size("tile")
    steps, pairs, _, width_all, ny = col.shape
    nx, width, _ = a_s.shape
    nf = width // hs_ref.shape[0]
    nl = hs_ref.shape[0]
    core = lev + 1 - 2 * (lev % 2)
    far = (lev + 2) % 4
    far_core = (core + 2) % 4

    loads = [
        pltpu.make_async_copy(jac_hbm, jac_s, load_sem.at[0]),
        pltpu.make_async_copy(perm_hbm, perm_s, load_sem.at[1]),
        pltpu.make_async_copy(frc_hbm, frc_s, load_sem.at[2]),
    ]
    for load in loads:
        load.start()

    barrier = pltpu.get_barrier_semaphore()

    def greet(l, d):
        pl.semaphore_signal(barrier, inc=1, device_id={"lev": l, "tile": d}, device_id_type=MESH)

    greet(core, t)
    greet(far, t)

    @pl.when(t > 0)
    def _():
        greet(lev, t - 1)

    @pl.when(t < n_tile - 1)
    def _():
        greet(lev, t + 1)

    for x in range(nx):
        a_s[x] = lam_ref[pl.ds(x, width, stride=nx), :]
        cx_s[x] = cx_ref[pl.ds(x, nl, stride=nx), :]
        cy_s[x] = cy_ref[pl.ds(x, nl, stride=nx), :]
    zero_e = jnp.zeros(east_in.shape[1:], F32)
    zero_w = jnp.zeros(west_in.shape[1:], F32)

    @pl.when(t == 0)
    def _():
        for n in range(steps):
            west_in[n] = zero_w

    @pl.when(t == n_tile - 1)
    def _():
        cxe_in[...] = jnp.zeros_like(cxe_in)
        for n in range(steps):
            east_in[n] = zero_e

    pl.semaphore_wait(barrier, 2 + (t > 0).astype(jnp.int32) + (t < n_tile - 1).astype(jnp.int32))

    def to_west(n):
        return pltpu.make_async_remote_copy(
            src_ref=edge_out.at[n], dst_ref=east_in.at[n], send_sem=es.at[n], recv_sem=er.at[n],
            device_id={"lev": lev, "tile": t - 1}, device_id_type=MESH,
        )

    def to_east(n):
        return pltpu.make_async_remote_copy(
            src_ref=rim_out.at[n], dst_ref=west_in.at[n], send_sem=ws.at[n], recv_sem=wr.at[n],
            device_id={"lev": lev, "tile": t + 1}, device_id_type=MESH,
        )

    cx_west = pltpu.make_async_remote_copy(
        src_ref=cx_s.at[0], dst_ref=cxe_in, send_sem=cs, recv_sem=cr,
        device_id={"lev": lev, "tile": t - 1}, device_id_type=MESH,
    )

    def send_halos(n, src):
        edge_out[n] = src[0]
        rim_out[n, :nl] = src[nx - 1, :nl]
        rim_out[n, nl:] = src[nx - 1, 3 * nl : 4 * nl]

        @pl.when(t > 0)
        def _():
            to_west(n).start()

        @pl.when(t < n_tile - 1)
        def _():
            to_east(n).start()

    @pl.when(t > 0)
    def _():
        cx_west.start()

    send_halos(0, a_s)

    def to_far(n, p):
        part = col.at[n, p, :, pl.ds(pl.multiple_of(lev * width, 16), width), :]
        return pltpu.make_async_remote_copy(
            src_ref=part, dst_ref=part, send_sem=zs.at[n, p], recv_sem=zr.at[n, p],
            device_id={"lev": far, "tile": t}, device_id_type=MESH,
        )

    def to_core(n, p):
        part = col.at[n, p, :, pl.ds(pl.multiple_of(lev * width, 16), width), :]
        return pltpu.make_async_remote_copy(
            src_ref=part, dst_ref=part, send_sem=ks.at[n, p], recv_sem=kr.at[n, p],
            device_id={"lev": core, "tile": t}, device_id_type=MESH,
        )

    def pass_on(n, p):
        part = col.at[n, p, :, pl.ds(pl.multiple_of(far * width, 16), width), :]
        return pltpu.make_async_remote_copy(
            src_ref=part, dst_ref=part, send_sem=fs.at[n, p], recv_sem=fr.at[n, p],
            device_id={"lev": core, "tile": t}, device_id_type=MESH,
        )

    hs = hs_ref[...]
    lane = iota((width, ny), 1)
    lane1 = iota((nl, ny), 1)

    def north(v):
        return jnp.where((lane if v.shape[0] == width else lane1) < ny - 1, pltpu.roll(v, ny - 1, axis=1), 0.0)

    def south(v):
        return jnp.where((lane if v.shape[0] == width else lane1) > 0, pltpu.roll(v, 1, axis=1), 0.0)

    def field(v, f):
        return v[f * nl : (f + 1) * nl]

    def dyn(n, x, src, dst):
        me = src[x]
        cx, cy = cx_s[x], cy_s[x]
        if x == nx - 1:
            east, cxe = east_in[n], cxe_in[...]
        else:
            east, cxe = src[x + 1], cx_s[x + 1]
        if x == 0:
            west_u, west_p = west_in[n, :nl], west_in[n, nl:]
        else:
            west_u, west_p = src[x - 1, :nl], src[x - 1, 3 * nl : 4 * nl]
        tile = lambda v: jnp.concatenate([v] * nf, axis=0)
        new = me + tile(cxe) * east + north(tile(cy) * me) - tile(cx + cy) * me
        v, p = field(me, 1), field(me, 3)
        d_u = hs * (field(east, 3) - west_p)
        d_v = hs * (north(p) - south(p))
        d_p = hs * (field(east, 0) - west_u + north(v) - south(v))
        zero = jnp.zeros_like(d_u)
        new = new + jnp.concatenate([d_u, d_v, zero, d_p, zero, zero], axis=0)
        dst[x] = new
        p_at, half = (x, 0) if x < pairs else (nx - 1 - x, 1)
        col[n, p_at, half, pl.ds(pl.multiple_of(lev * width, 16), width), :] = new.astype(BF)

    def phys(n, p, dst):
        to_far(n, p).wait_recv()
        pass_on(n, p).start()
        to_core(n, p).wait_recv()
        pass_on(n, p).wait_recv()
        both = jnp.concatenate([col[n, p, 0], col[n, p, 1]], axis=1)
        out = jnp.dot(jt_s[...], both, preferred_element_type=F32)
        for half, x in enumerate((p, nx - 1 - p)):
            part = out[:, half * ny : (half + 1) * ny]
            reg = reg_ref[n * nx + x : n * nx + x + 1, :]
            delta = part[:width]
            for r in range(1, part.shape[0] // width):
                delta = jnp.where(reg == r, part[r * width : (r + 1) * width], delta)
            dst[x] = dst[x] + delta.astype(BF).astype(F32) + frc_s[n, x]

    loads[0].wait()
    loads[1].wait()
    regimes = jac_s.shape[0]
    pick = perm_s[pl.ds(pl.multiple_of(lev * width, 16), width), :]
    for r in range(regimes):
        own = lax.dot_general(pick, jac_s[r], NT, preferred_element_type=F32).astype(BF)
        own = lax.dot_general(own, perm_s[...], NT, preferred_element_type=F32).astype(BF)
        jt_s[r * width : (r + 1) * width, :] = own
    loads[2].wait()

    def wait_halos(n):
        @pl.when(t < n_tile - 1)
        def _():
            to_west(n).wait_recv()

        @pl.when(t > 0)
        def _():
            to_east(n).wait_recv()

    def dyn_pair(n, p, src, dst):
        dyn(n, p, src, dst)
        dyn(n, nx - 1 - p, src, dst)
        to_far(n, p).start()
        to_core(n, p).start()

    @pl.when(t < n_tile - 1)
    def _():
        cx_west.wait_recv()

    wait_halos(0)
    for p in range(pairs):
        dyn_pair(0, p, a_s, b_s)
    now, new = b_s, a_s
    for n in range(steps):
        for p in range(pairs):
            phys(n, p, now)
            if n + 1 < steps:
                if p == 0:
                    send_halos(n + 1, now)
                if p == 1:
                    wait_halos(n + 1)
                if p >= 1:
                    dyn_pair(n + 1, p - 1, now, new)
        if n + 1 < steps:
            dyn_pair(n + 1, pairs - 1, now, new)
            now, new = new, now
    for x in range(nx):
        out_ref[pl.ds(x, width, stride=nx), :] = now[x]

    for n in range(steps):
        for p in range(pairs):
            to_far(n, p).wait_send()
            to_core(n, p).wait_send()
            pass_on(n, p).wait_send()

        @pl.when(t > 0)
        def _(n=n):
            to_west(n).wait_send()

        @pl.when(t < n_tile - 1)
        def _(n=n):
            to_east(n).wait_send()

    @pl.when(t > 0)
    def _():
        cx_west.wait_send()


def place_of(levels_all, lev_here, fields):
    dev, f, l = np.meshgrid(
        np.arange(levels_all // lev_here), np.arange(fields), np.arange(lev_here), indexing="ij"
    )
    place = (f * levels_all + dev * lev_here + l).reshape(-1)
    return (place[:, None] == np.arange(place.size)[None, :]).astype(np.float32)


def swept(lam, courant_x, courant_y, sound, phys_jac, regime, forcing, n_lev):
    fields, lev_here, nx, ny = lam.shape
    steps = regime.shape[0]
    regimes = phys_jac.shape[0]
    width = fields * lev_here
    width_all = width * n_lev
    pairs = nx // 2
    perm = jnp.asarray(place_of(lev_here * n_lev, lev_here, fields), BF)
    half = jnp.broadcast_to(0.5 * sound[:, None], (lev_here, ny))
    vmem = pl.BlockSpec(memory_space=pltpu.VMEM)
    hbm = pl.BlockSpec(memory_space=pl.ANY)
    dma = pltpu.SemaphoreType.DMA
    out = pl.pallas_call(
        step_kernel,
        out_shape=jax.ShapeDtypeStruct((width * nx, ny), F32),
        in_specs=[vmem, vmem, vmem, vmem, vmem, hbm, hbm, hbm],
        out_specs=vmem,
        scratch_shapes=[
            pltpu.VMEM((nx, width, ny), F32),
            pltpu.VMEM((nx, width, ny), F32),
            pltpu.VMEM((nx, lev_here, ny), F32),
            pltpu.VMEM((nx, lev_here, ny), F32),
            pltpu.VMEM((steps, nx, width, ny), F32),
            pltpu.VMEM((regimes, width_all, width_all), BF),
            pltpu.VMEM((width_all, width_all), BF),
            pltpu.VMEM((regimes * width, width_all), BF),
            pltpu.VMEM((steps, pairs, 2, width_all, ny), BF),
            pltpu.VMEM((steps, width, ny), F32),
            pltpu.VMEM((steps, 2 * lev_here, ny), F32),
            pltpu.VMEM((steps, width, ny), F32),
            pltpu.VMEM((steps, 2 * lev_here, ny), F32),
            pltpu.VMEM((lev_here, ny), F32),
            dma((3,)),
            dma((steps, pairs)), dma((steps, pairs)), dma((steps, pairs)),
            dma((steps, pairs)), dma((steps, pairs)), dma((steps, pairs)),
            dma((steps,)), dma((steps,)), dma((steps,)), dma((steps,)), dma, dma,
        ],
        compiler_params=pltpu.CompilerParams(
            collective_id=1, has_side_effects=True, vmem_limit_bytes=56 * 1024 * 1024
        ),
        name="sweep",
    )(
        lam.reshape(width * nx, ny),
        courant_x.reshape(lev_here * nx, ny),
        courant_y.reshape(lev_here * nx, ny),
        half,
        regime.reshape(steps * nx, ny),
        forcing,
        phys_jac,
        perm,
    )
    return out.reshape(lam.shape)


def on_device(
    adjoint_final,
    courant_x,
    courant_y,
    sound,
    phys_jac,
    regime,
    obs_operator,
    obs_rows,
    obs_owner,
    obs_cell,
    obs_count,
):
    fields, lev_here, cols_x, cols_y = adjoint_final.shape
    n_tile = lax.axis_size("tile")
    n_lev = lax.axis_size("lev")
    forcing = forcing_of(
        obs_operator, obs_rows, obs_owner, obs_cell, obs_count, n_tile, cols_x * cols_y
    )
    return swept(adjoint_final, courant_x, courant_y, sound, phys_jac, regime, forcing, n_lev)


def solution(mesh):
    return jax.shard_map(
        on_device,
        mesh=mesh,
        in_specs=(
            P(None, "lev", "tile", None),
            P("lev", "tile", None),
            P("lev", "tile", None),
            P("lev"),
            P(),
            P(None, "tile", None),
            P(None, None, "lev"),
            P(None, "tile", None),
            P(None, "tile", None),
            P(None, "tile"),
            P(None, "tile"),
        ),
        out_specs=P(None, "lev", "tile", None),
        check_vma=False,
    )
```

```python
import jax
import jax.numpy as jnp
import numpy as np
from jax import lax
from jax.experimental import pallas as pl
from jax.experimental.pallas import tpu as pltpu
from jax.sharding import PartitionSpec as P

MESH = pl.DeviceIdType.MESH
BF = jnp.bfloat16
F32 = jnp.float32
NT = (((1,), (1,)), ((), ()))
GROUP = 8


def iota(shape, dim):
    return lax.broadcasted_iota(jnp.int32, shape, dim)


def owner_lev(t, d, lev, per_z):
    h = lev // 2
    c = lev % 2
    apart = jnp.abs(t // per_z - d // per_z)
    return jnp.where(apart == 3, 1 - h, h) * 2 + c


def kernel(
    lam_ref, cx_ref, cy_ref, sound_ref, reg_ref, op_ref, own_ref, cell_ref, cnt_ref,
    jac_hbm, perm_hbm, rows_hbm, out_ref,
    rows_v, send_rows, recv_rows, send_cell, recv_cell, oh, rc, rank_s, own_s, pmat, key_s, ohs, acc, g_s,
    a_s, b_s, lam_out, misc, misc_out, op_s, jac_s, perm_s, jt_s, col,
    e_in, w_in, e_out, w_out, cxe_in, cxe_out, fin_in,
    load_sem, ss_rows, rs_rows, ss_cell, rs_cell, gs_sem, gr_sem,
    xs_sem, xr_sem, es, er, ws, wr, cs, cr, ks, kr, ts, tr,
):
    lev = lax.axis_index("lev")
    t = lax.axis_index("tile")
    _, n_tile, cap, vals = send_rows.shape
    obs = rows_v.shape[1]
    per_z = n_tile // 4
    h = lev // 2
    c = lev % 2
    core = lev + 1 - 2 * c
    far = (lev + 2) % 4
    steps, half_x, width_all, ny = col.shape
    nx = 2 * half_x
    width = a_s.shape[2]
    nl = misc.shape[2]
    nf = width // nl
    low = h == t % 2
    x0 = jnp.where(low, 0, half_x)
    x1 = half_x - x0
    groups = n_tile // GROUP
    my_group = t // GROUP
    own_rows = pl.ds(pl.multiple_of(c * 2 * width, 16), 2 * width)

    w_lev, w_tile = jnp.where(low, lev, far), jnp.where(low, t - 1, t)
    e_lev, e_tile = jnp.where(low, far, lev), jnp.where(low, t, t + 1)
    has_west = w_tile >= 0
    has_east = e_tile < n_tile

    def remote(src, dst, ssem, rsem, to_lev, to_tile):
        return pltpu.make_async_remote_copy(
            src_ref=src, dst_ref=dst, send_sem=ssem, recv_sem=rsem,
            device_id={"lev": to_lev, "tile": to_tile}, device_id_type=MESH,
        )

    load_rows = [
        pltpu.make_async_copy(rows_hbm.at[c + 2 * j], rows_v.at[j], load_sem.at[j]) for j in range(2)
    ]
    load_jac = pltpu.make_async_copy(jac_hbm, jac_s, load_sem.at[2])
    load_perm = pltpu.make_async_copy(perm_hbm, perm_s, load_sem.at[3])
    for load in load_rows + [load_jac, load_perm]:
        load.start()

    barrier = pltpu.get_barrier_semaphore()

    def greet(i, _):
        d = (t + i) % n_tile
        pl.semaphore_signal(
            barrier, inc=1, device_id={"lev": owner_lev(t, d, lev, per_z), "tile": d}, device_id_type=MESH
        )
        return 0

    lax.fori_loop(1, n_tile, greet, 0)
    for other in (core, far):
        pl.semaphore_signal(barrier, inc=1, device_id={"lev": other, "tile": t}, device_id_type=MESH)

    def columns(ref, x, rows):
        return ref[pl.ds(x, rows, stride=nx), :]

    same = iota((nl, nl), 0) == iota((nl, nl), 1)
    hs = 0.5 * jnp.sum(jnp.where(same, sound_ref[...], 0.0), axis=1, keepdims=True)
    hs = jnp.broadcast_to(hs, (nl, ny))
    for i in range(half_x):
        lam_out[i] = columns(lam_ref, x1 + i, width)
        misc_out[i] = columns(cx_ref, x1 + i, nl)
        misc_out[half_x + i] = columns(cy_ref, x1 + i, nl)
        a_s[i, h] = columns(lam_ref, x0 + i, width)
        misc[h, i] = columns(cx_ref, x0 + i, nl)
        misc[h, half_x + i] = columns(cy_ref, x0 + i, nl)
    for ref in (misc_out, misc.at[h]):
        ref[nx] = hs
        ref[nx + 1] = columns(cx_ref, half_x, nl)
    op_s[h] = op_ref[...]

    cx_goes = jnp.logical_and(low, has_west)
    cx_comes = jnp.logical_and(jnp.logical_not(low), has_east)

    @pl.when(jnp.logical_not(cx_comes))
    def _():
        cxe_in[...] = jnp.zeros_like(cxe_in)

    @pl.when(jnp.logical_not(has_west))
    def _():
        w_in[...] = jnp.zeros_like(w_in)

    @pl.when(jnp.logical_not(has_east))
    def _():
        e_in[...] = jnp.zeros_like(e_in)

    pl.semaphore_wait(barrier, n_tile + 1)

    order = [0, half_x - 1] + list(range(1, half_x - 1))
    swap_misc = remote(misc_out, misc.at[h], xs_sem.at[half_x], xr_sem.at[half_x], far, t)
    swap_op = remote(op_s.at[h], op_s.at[h], xs_sem.at[half_x + 1], xr_sem.at[half_x + 1], far, t)
    swap_lam = [remote(lam_out.at[i], a_s.at[i, h], xs_sem.at[i], xr_sem.at[i], far, t) for i in range(half_x)]
    swap_misc.start()
    for i in order:
        swap_lam[i].start()
    swap_op.start()

    upper = jnp.where(iota((128, 256), 0) < iota((128, 256), 1), 1.0, 0.0).astype(BF)
    lane128 = iota((n_tile, 128), 1)

    def rank_rows(j):
        step = c + 2 * j
        live = iota((1, obs), 1) < cnt_ref[0, step]
        own = jnp.where(live, own_ref[step], -1)
        own_s[j] = own
        oh[...] = jnp.where(own == iota((n_tile, obs), 0), 1.0, 0.0).astype(BF)
        carry = jnp.zeros((n_tile, 128), F32)
        for b in range(obs // 128):
            cols = slice(b * 128, (b + 1) * 128)
            hot = oh[:, cols]
            ex = jnp.dot(hot, upper, preferred_element_type=F32)
            rank_s[j, :, cols] = jnp.sum(hot.astype(F32) * (ex[:, :128] + carry), axis=0, keepdims=True)
            carry = carry + ex[:, 128:]
        rank = jnp.where(live, rank_s[j], -1.0)
        rank_s[j] = rank
        cell = cell_ref[pl.ds(step, 1), :]
        hot = rank == iota((cap, obs), 0).astype(F32)
        rc[:cap] = jnp.where(hot, (cell >> 7).astype(F32), 0.0).astype(BF)
        rc[cap:] = jnp.where(hot, ((cell & 127) + 1).astype(F32), 0.0).astype(BF)
        both = lax.dot_general(oh[...], rc[...], NT, preferred_element_type=F32)
        key = both * 128.0 + pltpu.roll(both, 64, axis=1)
        return jnp.where(lane128 < 64, key, 0.0)

    def cell_copy(d):
        return remote(
            send_cell.at[pl.ds(d, 1), :], recv_cell.at[pl.ds(t, 1), :], ss_cell.at[d], rs_cell.at[t],
            owner_lev(t, d, lev, per_z), d,
        )

    def row_copy(j, d):
        return remote(
            send_rows.at[j, d], recv_rows.at[j, t], ss_rows.at[j, d], rs_rows.at[j, t],
            owner_lev(t, d, lev, per_z), d,
        )

    def arrival(buf, sem, s):
        return remote(buf, buf, sem, sem, owner_lev(t, s, lev, per_z), s)

    sub16 = iota((16, obs), 0).astype(F32)

    def pack_rows(j):
        load_rows[j].wait()

        def pack(g, _):
            d0 = pl.multiple_of(((g + my_group) % groups) * GROUP, GROUP)
            for i in range(GROUP):
                key = jnp.where(own_s[j] == d0 + i, rank_s[j], -1.0)
                key = jnp.broadcast_to(key, (16, obs)).astype(BF)
                for q in range(cap // 16):
                    hot = key == (sub16 + 16.0 * q).astype(BF)
                    pmat[i * cap + q * 16 : i * cap + (q + 1) * 16, :] = jnp.where(
                        hot, jnp.ones((), BF), jnp.zeros((), BF)
                    )
            packed = jnp.dot(pmat[...], rows_v[j], preferred_element_type=F32)
            send_rows[j, pl.ds(d0, GROUP)] = packed.astype(BF).reshape(GROUP, cap, vals)

            def send(i, _):
                d = d0 + i

                @pl.when(d != t)
                def _():
                    row_copy(j, d).start()

                return 0

            lax.fori_loop(0, GROUP, send, 0)
            return 0

        lax.fori_loop(0, groups, pack, 0)
        recv_rows[j, t] = send_rows[j, t]

    key0 = rank_rows(0)
    pack_rows(0)
    send_cell[...] = key0 + pltpu.roll(rank_rows(1), 64, axis=1)

    def send_cells(i, _):
        cell_copy((t + i) % n_tile).start()
        return 0

    lax.fori_loop(1, n_tile, send_cells, 0)
    recv_cell[pl.ds(t, 1), :] = send_cell[pl.ds(t, 1), :]

    def to_west(n):
        return remote(e_out.at[n], e_in.at[n], es.at[n], er.at[n], w_lev, w_tile)

    def to_east(n):
        return remote(w_out.at[n], w_in.at[n], ws.at[n], wr.at[n], e_lev, e_tile)

    cx_west = remote(cxe_out, cxe_in, cs, cr, w_lev, w_tile)

    def send_halos(n, src):
        for b in range(2):
            e_out[n, b] = src[0, b].astype(BF)
            last = src[half_x - 1, b]
            w_out[n, b] = jnp.concatenate([last[:nl], last[3 * nl : 4 * nl]], axis=0).astype(BF)

        @pl.when(has_west)
        def _():
            to_west(n).start()

        @pl.when(has_east)
        def _():
            to_east(n).start()

    def wait_halos(n):
        @pl.when(has_east)
        def _():
            to_west(n).wait_recv()

        @pl.when(has_west)
        def _():
            to_east(n).wait_recv()

    swap_misc.wait_recv()
    for i in (0, half_x - 1):
        swap_lam[i].wait_recv()
    for b in range(2):
        cxe_out[b] = misc[b, 0]
    @pl.when(cx_goes)
    def _():
        cx_west.start()

    send_halos(0, a_s)

    load_jac.wait()
    load_perm.wait()
    regimes = jac_s.shape[0]
    for r in range(regimes):
        mine = lax.dot_general(perm_s[own_rows, :], jac_s[r], NT, preferred_element_type=F32).astype(BF)
        mine = lax.dot_general(mine, perm_s[...], NT, preferred_element_type=F32).astype(BF)
        jt_s[r * 2 * width : (r + 1) * 2 * width, :] = mine

    pack_rows(1)

    lane = iota((width, ny), 1)
    lane1 = iota((nl, ny), 1)

    def north(v):
        inside = (lane if v.shape[0] == width else lane1) < ny - 1
        return jnp.where(inside, pltpu.roll(v, ny - 1, axis=1), 0.0)

    def south(v):
        inside = (lane if v.shape[0] == width else lane1) > 0
        return jnp.where(inside, pltpu.roll(v, 1, axis=1), 0.0)

    def field(v, f):
        return v[f * nl : (f + 1) * nl]

    def to_core(n, x):
        part = col.at[n, x, own_rows, :]
        return remote(part, part, ks.at[n, x], kr.at[n, x], core, t)

    def dyn(n, x, src, dst):
        for b in range(2):
            me = src[x, b]
            cx, cy, hl = misc[b, x], misc[b, half_x + x], misc[b, nx]
            if x == half_x - 1:
                east = e_in[n, b].astype(F32)
                cxe = jnp.where(low, misc[b, nx + 1], cxe_in[b])
            else:
                east, cxe = src[x + 1, b], misc[b, x + 1]
            if x == 0:
                west = w_in[n, b].astype(F32)
                west_u, west_p = west[:nl], west[nl:]
            else:
                west_u, west_p = src[x - 1, b, :nl], src[x - 1, b, 3 * nl : 4 * nl]
            tile = lambda v: jnp.concatenate([v] * nf, axis=0)
            new = me + tile(cxe) * east + north(tile(cy) * me) - tile(cx + cy) * me
            v, p = field(me, 1), field(me, 3)
            d_u = hl * (field(east, 3) - west_p)
            d_v = hl * (north(p) - south(p))
            d_p = hl * (field(east, 0) - west_u + north(v) - south(v))
            zero = jnp.zeros_like(d_u)
            new = new + jnp.concatenate([d_u, d_v, zero, d_p, zero, zero], axis=0)
            dst[x, b] = new
            col[n, x, pl.ds(pl.multiple_of(c * 2 * width + b * width, 16), width), :] = new.astype(BF)
        to_core(n, x).start()

    def phys(n, xs, dst):
        for x in xs:
            to_core(n, x).wait_recv()
        both = jnp.concatenate([col[n, x] for x in xs], axis=1)
        out = jnp.dot(jt_s[...], both, preferred_element_type=F32)
        ops = [jnp.concatenate([op_s[b], op_s[b]], axis=1) for b in range(2)]
        for at, x in enumerate(xs):
            part = out[:, at * ny : (at + 1) * ny]
            reg = reg_ref[pl.ds(n * nx + x0 + x, 1), :]
            sums = g_s[n, x * ny : (x + 1) * ny, :]
            for b in range(2):
                delta = part[b * width : (b + 1) * width]
                for r in range(1, regimes):
                    row = (2 * r + b) * width
                    delta = jnp.where(reg == r, part[row : row + width], delta)
                forcing = lax.dot_general(ops[b], sums, NT, preferred_element_type=F32)
                dst[x, b] = dst[x, b] + delta.astype(BF).astype(F32) + forcing

    def cells_in(i, _):
        s = (t + n_tile - i) % n_tile
        arrival(recv_cell.at[pl.ds(s, 1), :], rs_cell.at[s], s).wait_recv()
        return 0

    def read_cells():
        lax.fori_loop(1, n_tile, cells_in, 0)
        even = recv_cell[pl.ds(0, n_tile // 2, stride=2), :]
        odd = recv_cell[pl.ds(1, n_tile // 2, stride=2), :]
        left = iota((n_tile // 2, 128), 1) < 64
        key_s[0] = jnp.where(left, even, pltpu.roll(odd, 64, axis=1)).astype(jnp.int32) - 1
        key_s[1] = jnp.where(left, pltpu.roll(even, 64, axis=1), odd).astype(jnp.int32) - 1

    sub16s = iota((16, GROUP * cap), 0).astype(F32)

    def sum_rows(j, first, last):
        def unpack(g, _):
            s0 = pl.multiple_of(((groups - g + my_group) % groups) * GROUP, GROUP)

            def take(i, _):
                s = s0 + i

                @pl.when(s != t)
                def _():
                    arrival(recv_rows.at[j, s], rs_rows.at[j, s], s).wait_recv()

                return 0

            lax.fori_loop(0, GROUP, take, 0)
            key = jnp.concatenate(
                [key_s[j, pl.ds(s0 // 2 + q, 1), :] for q in range(GROUP // 2)], axis=1
            )
            at_x = (key >> 7) - x0
            at_y = (key & 127).astype(F32)
            for x in range(half_x):
                kx = jnp.broadcast_to(jnp.where(at_x == x, at_y, -1.0), (16, GROUP * cap)).astype(BF)
                for q in range(ny // 16):
                    hot = kx == (sub16s + 16.0 * q).astype(BF)
                    ohs[x * ny + q * 16 : x * ny + (q + 1) * 16, :] = jnp.where(
                        hot, jnp.ones((), BF), jnp.zeros((), BF)
                    )
            rows = recv_rows[j, pl.ds(s0, GROUP)].reshape(GROUP * cap, vals)
            acc[...] += jnp.dot(ohs[...], rows, preferred_element_type=F32)
            return 0

        if first == 0:
            acc[...] = jnp.zeros_like(acc)
        lax.fori_loop(first, last, unpack, 0)

    def share(j):
        part = g_s.at[c + 2 * j]
        return remote(part, part, gs_sem.at[j], gr_sem.at[j], core, t)

    def share_sums(j):
        total = acc[...]
        head = total.astype(BF)
        g_s[c + 2 * j, :, :vals] = head
        g_s[c + 2 * j, :, vals:] = (total - head.astype(F32)).astype(BF)
        share(j).start()

    for i in range(1, half_x - 1):
        swap_lam[i].wait_recv()

    @pl.when(cx_comes)
    def _():
        cx_west.wait_recv()

    inner = list(range(1, half_x - 1))
    outer = [0, half_x - 1]
    for x in inner:
        dyn(0, x, a_s, b_s)
    wait_halos(0)
    for x in outer:
        dyn(0, x, a_s, b_s)
    read_cells()
    sum_rows(0, 0, groups)
    share_sums(0)
    swap_op.wait_recv()
    now, new = b_s, a_s
    for n in range(steps):
        if n == 0:
            share(0).wait_recv()
        if n == 2:
            share(1).wait_recv()
        phys(n, outer, now)
        if n + 1 < steps:
            send_halos(n + 1, now)
        else:
            finish(outer, now, fin_in, ts, tr, h, far, t, remote)
        phys(n, inner, now)
        if n + 1 == steps:
            finish(inner, now, fin_in, ts, tr, h, far, t, remote)
            break
        if n == 0:
            sum_rows(1, 0, groups // 2)
        if n == 1:
            sum_rows(1, groups // 2, groups)
            share_sums(1)
        for x in inner:
            dyn(n + 1, x, now, new)
        wait_halos(n + 1)
        for x in outer:
            dyn(n + 1, x, now, new)
        now, new = new, now

    for i in range(half_x):
        out_ref[pl.ds(x0 + i, width, stride=nx), :] = now[i, h]
    for i in outer + inner:
        remote(now.at[i, 1 - h], fin_in.at[i], ts.at[i], tr.at[i], far, t).wait_recv()
        out_ref[pl.ds(x1 + i, width, stride=nx), :] = fin_in[i]

    def drain(i, _):
        d = (t + i) % n_tile
        cell_copy(d).wait_send()
        for j in range(2):
            row_copy(j, d).wait_send()
        return 0

    lax.fori_loop(1, n_tile, drain, 0)
    for copy in [swap_misc, swap_op] + swap_lam + [share(0), share(1)]:
        copy.wait_send()

    @pl.when(cx_goes)
    def _():
        cx_west.wait_send()

    for i in range(half_x):
        remote(now.at[i, 1 - h], fin_in.at[i], ts.at[i], tr.at[i], far, t).wait_send()
    for n in range(steps):
        for x in range(half_x):
            to_core(n, x).wait_send()

        @pl.when(has_west)
        def _(n=n):
            to_west(n).wait_send()

        @pl.when(has_east)
        def _(n=n):
            to_east(n).wait_send()


def finish(xs, now, fin_in, ts, tr, h, far, t, remote):
    for x in xs:
        remote(now.at[x, 1 - h], fin_in.at[x], ts.at[x], tr.at[x], far, t).start()


def place_of(levels_all, lev_here, fields):
    core, far, f, l = np.meshgrid(
        np.arange(2), np.arange(2), np.arange(fields), np.arange(lev_here), indexing="ij"
    )
    place = (f * levels_all + (2 * far + core) * lev_here + l).reshape(-1)
    return (place[:, None] == np.arange(place.size)[None, :]).astype(np.float32)


def on_device(
    adjoint_final,
    courant_x,
    courant_y,
    sound,
    phys_jac,
    regime,
    obs_operator,
    obs_rows,
    obs_owner,
    obs_cell,
    obs_count,
):
    fields, nl, nx, ny = adjoint_final.shape
    n_tile = lax.axis_size("tile")
    n_lev = lax.axis_size("lev")
    steps, obs, vals = obs_rows.shape
    cap = max(2, 2 * obs // n_tile)
    regimes = phys_jac.shape[0]
    width = fields * nl
    width_all = width * n_lev
    hx = nx // 2
    perm = jnp.asarray(place_of(nl * n_lev, nl, fields), BF)
    vmem = pl.BlockSpec(memory_space=pltpu.VMEM)
    hbm = pl.BlockSpec(memory_space=pl.ANY)
    V = pltpu.VMEM
    dma = pltpu.SemaphoreType.DMA
    out = pl.pallas_call(
        kernel,
        out_shape=jax.ShapeDtypeStruct((width * nx, ny), F32),
        in_specs=[vmem] * 8 + [pl.BlockSpec(memory_space=pltpu.SMEM)] + [hbm] * 3,
        out_specs=vmem,
        scratch_shapes=[
            V((2, obs, vals), BF),
            V((2, n_tile, cap, vals), BF),
            V((2, n_tile, cap, vals), BF),
            V((n_tile, 128), F32),
            V((n_tile, 128), F32),
            V((n_tile, obs), BF),
            V((2 * cap, obs), BF),
            V((2, 1, obs), F32),
            V((2, 1, obs), jnp.int32),
            V((GROUP * cap, obs), BF),
            V((2, n_tile // 2, 128), jnp.int32),
            V((hx * ny, GROUP * cap), BF),
            V((hx * ny, vals), F32),
            V((steps, hx * ny, 2 * vals), BF),
            V((hx, 2, width, ny), F32),
            V((hx, 2, width, ny), F32),
            V((hx, width, ny), F32),
            V((2, nx + 2, nl, ny), F32),
            V((nx + 2, nl, ny), F32),
            V((2, width, vals), BF),
            V((regimes, width_all, width_all), BF),
            V((width_all, width_all), BF),
            V((regimes * 2 * width, width_all), BF),
            V((steps, hx, width_all, ny), BF),
            V((steps, 2, width, ny), BF),
            V((steps, 2, 2 * nl, ny), BF),
            V((steps, 2, width, ny), BF),
            V((steps, 2, 2 * nl, ny), BF),
            V((2, nl, ny), F32),
            V((2, nl, ny), F32),
            V((hx, width, ny), F32),
            dma((4,)), dma((2, n_tile)), dma((2, n_tile)), dma((n_tile,)), dma((n_tile,)), dma((2,)), dma((2,)),
            dma((hx + 2,)), dma((hx + 2,)), dma((steps,)), dma((steps,)), dma((steps,)), dma((steps,)),
            dma, dma, dma((steps, hx)), dma((steps, hx)), dma((hx,)), dma((hx,)),
        ],
        compiler_params=pltpu.CompilerParams(
            collective_id=0, has_side_effects=True, vmem_limit_bytes=56 * 1024 * 1024
        ),
        name="sweep",
    )(
        adjoint_final.reshape(width * nx, ny),
        courant_x.reshape(nl * nx, ny),
        courant_y.reshape(nl * nx, ny),
        sound.reshape(1, nl),
        regime.reshape(steps * nx, ny),
        obs_operator.transpose(1, 2, 0).reshape(width, vals),
        obs_owner.reshape(steps, 1, obs),
        obs_cell,
        obs_count.reshape(1, steps),
        phys_jac,
        perm,
        obs_rows,
    )
    return out.reshape(adjoint_final.shape)


def solution(mesh):
    return jax.shard_map(
        on_device,
        mesh=mesh,
        in_specs=(
            P(None, "lev", "tile", None),
            P("lev", "tile", None),
            P("lev", "tile", None),
            P("lev"),
            P(),
            P(None, "tile", None),
            P(None, None, "lev"),
            P(None, "tile", None),
            P(None, "tile", None),
            P(None, "tile"),
            P(None, "tile"),
        ),
        out_specs=P(None, "lev", "tile", None),
        check_vma=False,
    )
```

```python
import jax
import jax.numpy as jnp
import numpy as np
from jax import lax
from jax.experimental import pallas as pl
from jax.experimental.pallas import tpu as pltpu
from jax.sharding import PartitionSpec as P

MESH = pl.DeviceIdType.MESH
BF = jnp.bfloat16
F32 = jnp.float32
NT = (((1,), (1,)), ((), ()))
GROUP = 8


def iota(shape, dim):
    return lax.broadcasted_iota(jnp.int32, shape, dim)


def crosses(t, d, n_tile):
    per_z = n_tile // 4
    apart = jnp.abs(t // per_z - d // per_z)
    odd = (t // GROUP + d // GROUP) % 2 == 1
    return jnp.logical_or(apart == 3, jnp.logical_and(apart == 2, odd))


def kernel(
    sound_ref, reg_ref, op_ref, own_ref, cell_ref, cnt_ref,
    lam_hbm, cx_hbm, cy_hbm, jac_hbm, perm_hbm, rows_hbm, out_hbm,
    lam_ref, cx_ref, cy_ref,
    rows_v, send_rows, recv_rows, send_cell, recv_cell, oh, rc, rank_s, own_s, pmat, key_s, ohs, acc, g_s, g_far,
    a_s, b_s, lam_out, misc, misc_out, op_s, jac_s, perm_s, jt_s, col,
    e_in, w_in, e_out, w_out, cxe_in, cxe_out,
    load_sem, ss_rows, rs_rows, ss_cell, rs_cell, gks, gkr, gzs, gzr, gfs, gfr,
    xs_sem, xr_sem, es, er, ws, wr, cs, cr, ks, kr, ts, tr, ls,
):
    lev = lax.axis_index("lev")
    t = lax.axis_index("tile")
    n_tile, cap, vals = send_rows.shape
    obs = rows_v.shape[1]
    h = lev // 2
    c = lev % 2
    core = lev + 1 - 2 * c
    far = (lev + 2) % 4
    steps, half_x, width_all, ny = col.shape
    nx = 2 * half_x
    width = a_s.shape[2]
    nl = misc.shape[2]
    nf = width // nl
    low = h == t % 2
    x0 = jnp.where(low, 0, half_x)
    x1 = half_x - x0
    groups = n_tile // GROUP
    my_group = t // GROUP
    own_rows = pl.ds(pl.multiple_of(c * 2 * width, 16), 2 * width)

    w_lev, w_tile = jnp.where(low, lev, far), jnp.where(low, t - 1, t)
    e_lev, e_tile = jnp.where(low, far, lev), jnp.where(low, t, t + 1)
    has_west = w_tile >= 0
    has_east = e_tile < n_tile

    def remote(src, dst, ssem, rsem, to_lev, to_tile):
        return pltpu.make_async_remote_copy(
            src_ref=src, dst_ref=dst, send_sem=ssem, recv_sem=rsem,
            device_id={"lev": to_lev, "tile": to_tile}, device_id_type=MESH,
        )

    mine = lev
    sent_steps = (lev, far)
    load_rows = [pltpu.make_async_copy(rows_hbm.at[n], rows_v.at[j], load_sem.at[j]) for j, n in enumerate(sent_steps)]
    load_jac = pltpu.make_async_copy(jac_hbm, jac_s, load_sem.at[2])
    load_perm = pltpu.make_async_copy(perm_hbm, perm_s, load_sem.at[6])
    load_state = [
        pltpu.make_async_copy(src, dst, load_sem.at[3 + i])
        for i, (src, dst) in enumerate(((lam_hbm, lam_ref), (cx_hbm, cx_ref), (cy_hbm, cy_ref)))
    ]
    for load in load_state + load_rows + [load_jac, load_perm]:
        load.start()

    barrier = pltpu.get_barrier_semaphore()

    def greet(i, _):
        d = (t + i) % n_tile
        pl.semaphore_signal(
            barrier, inc=1, device_id={"lev": jnp.where(crosses(t, d, n_tile), far, lev), "tile": d}, device_id_type=MESH
        )
        return 0

    lax.fori_loop(1, n_tile, greet, 0)
    for other in (core, far):
        pl.semaphore_signal(barrier, inc=1, device_id={"lev": other, "tile": t}, device_id_type=MESH)

    def columns(ref, x, rows):
        return ref[pl.ds(x, rows, stride=nx), :]

    same = iota((nl, nl), 0) == iota((nl, nl), 1)
    hs = 0.5 * jnp.sum(jnp.where(same, sound_ref[...], 0.0), axis=1, keepdims=True)
    hs = jnp.broadcast_to(hs, (nl, ny))
    for load in load_state:
        load.wait()
    for i in range(half_x):
        lam_out[i] = columns(lam_ref, x1 + i, width)
        misc_out[i] = columns(cx_ref, x1 + i, nl)
        misc_out[half_x + i] = columns(cy_ref, x1 + i, nl)
        a_s[i, h] = columns(lam_ref, x0 + i, width)
        misc[h, i] = columns(cx_ref, x0 + i, nl)
        misc[h, half_x + i] = columns(cy_ref, x0 + i, nl)
    for ref in (misc_out, misc.at[h]):
        ref[nx] = hs
        ref[nx + 1] = columns(cx_ref, half_x, nl)
    op_s[h] = op_ref[...]

    cx_goes = jnp.logical_and(low, has_west)
    cx_comes = jnp.logical_and(jnp.logical_not(low), has_east)

    @pl.when(jnp.logical_not(cx_comes))
    def _():
        cxe_in[...] = jnp.zeros_like(cxe_in)

    @pl.when(jnp.logical_not(has_west))
    def _():
        w_in[...] = jnp.zeros_like(w_in)

    @pl.when(jnp.logical_not(has_east))
    def _():
        e_in[...] = jnp.zeros_like(e_in)

    pl.semaphore_wait(barrier, n_tile + 1)

    inner = list(range(1, half_x - 1))
    outer = [0, half_x - 1]
    order = outer + inner
    slot = {x: i for i, x in enumerate(order)}
    swap_misc = remote(misc_out, misc.at[h], xs_sem.at[half_x], xr_sem.at[half_x], far, t)
    swap_op = remote(op_s.at[h], op_s.at[h], xs_sem.at[half_x + 1], xr_sem.at[half_x + 1], far, t)
    swap_lam = [remote(lam_out.at[i], a_s.at[i, h], xs_sem.at[i], xr_sem.at[i], far, t) for i in range(half_x)]
    swap_misc.start()
    for i in order:
        swap_lam[i].start()
    swap_op.start()

    upper = jnp.where(iota((128, 256), 0) < iota((128, 256), 1), 1.0, 0.0).astype(BF)
    lane128 = iota((n_tile, 128), 1)

    def rank_rows(j):
        step = sent_steps[j]
        live = iota((1, obs), 1) < cnt_ref[0, step]
        own = jnp.where(live, own_ref[step], -1)
        own_s[j] = own
        oh[...] = jnp.where(own == iota((n_tile, obs), 0), 1.0, 0.0).astype(BF)
        carry = jnp.zeros((n_tile, 128), F32)
        for b in range(obs // 128):
            cols = slice(b * 128, (b + 1) * 128)
            hot = oh[:, cols]
            ex = jnp.dot(hot, upper, preferred_element_type=F32)
            rank_s[j, :, cols] = jnp.sum(hot.astype(F32) * (ex[:, :128] + carry), axis=0, keepdims=True)
            carry = carry + ex[:, 128:]
        rank = jnp.where(live, rank_s[j], -1.0)
        rank_s[j] = rank
        cell = cell_ref[pl.ds(step, 1), :]
        hot = rank == iota((cap, obs), 0).astype(F32)
        rc[:cap] = jnp.where(hot, (cell >> 7).astype(F32), 0.0).astype(BF)
        rc[cap:] = jnp.where(hot, ((cell & 127) + 1).astype(F32), 0.0).astype(BF)
        both = lax.dot_general(oh[...], rc[...], NT, preferred_element_type=F32)
        key = both * 128.0 + pltpu.roll(both, 64, axis=1)
        return jnp.where(lane128 < 64, key, 0.0)

    def cell_copy(d):
        return remote(
            send_cell.at[crosses(t, d, n_tile).astype(jnp.int32), pl.ds(d, 1), :], recv_cell.at[pl.ds(t, 1), :],
            ss_cell, rs_cell, jnp.where(crosses(t, d, n_tile), far, lev), d,
        )

    def row_copy(d):
        return remote(
            send_rows.at[d], recv_rows.at[t], ss_rows, rs_rows.at[my_group],
            jnp.where(crosses(t, d, n_tile), far, lev), d,
        )

    def all_of(buf, ssem, rsem):
        return remote(buf, buf, ssem, rsem, far, t)

    sub16 = iota((16, obs), 0).astype(F32)

    def pack_rows():
        for load in load_rows:
            load.wait()

        def pack(g, _):
            d0 = pl.multiple_of(((g + my_group) % groups) * GROUP, GROUP)
            j = crosses(t, d0, n_tile).astype(jnp.int32)
            for i in range(GROUP):
                key = jnp.where(own_s[j] == d0 + i, rank_s[j], -1.0)
                key = jnp.broadcast_to(key, (16, obs)).astype(BF)
                for q in range(cap // 16):
                    hot = key == (sub16 + 16.0 * q).astype(BF)
                    pmat[i * cap + q * 16 : i * cap + (q + 1) * 16, :] = jnp.where(
                        hot, jnp.ones((), BF), jnp.zeros((), BF)
                    )
            packed = jnp.dot(pmat[...], rows_v[j], preferred_element_type=F32)
            send_rows[pl.ds(d0, GROUP)] = packed.astype(BF).reshape(GROUP, cap, vals)

            def send(i, _):
                d = d0 + i

                @pl.when(d != t)
                def _():
                    row_copy(d).start()

                return 0

            lax.fori_loop(0, GROUP, send, 0)
            return 0

        lax.fori_loop(0, groups, pack, 0)
        recv_rows[t] = send_rows[t]

    for j in range(2):
        keys = rank_rows(j)
        send_cell[j] = jnp.where(t % 2 == 0, keys, pltpu.roll(keys, 64, axis=1))

    def send_cells(i, _):
        cell_copy((t + i) % n_tile).start()
        return 0

    lax.fori_loop(1, n_tile, send_cells, 0)
    recv_cell[pl.ds(t, 1), :] = send_cell[0, pl.ds(t, 1), :]
    pack_rows()

    def to_west(n):
        return remote(e_out.at[n], e_in.at[n], es.at[n], er.at[n], w_lev, w_tile)

    def to_east(n):
        return remote(w_out.at[n], w_in.at[n], ws.at[n], wr.at[n], e_lev, e_tile)

    cx_west = remote(cxe_out, cxe_in, cs, cr, w_lev, w_tile)

    def send_halos(n, src):
        for b in range(2):
            e_out[n, b] = src[0, b].astype(BF)
            last = src[half_x - 1, b]
            w_out[n, b] = jnp.concatenate([last[:nl], last[3 * nl : 4 * nl]], axis=0).astype(BF)

        @pl.when(has_west)
        def _():
            to_west(n).start()

        @pl.when(has_east)
        def _():
            to_east(n).start()

    def wait_halos(n):
        @pl.when(has_east)
        def _():
            to_west(n).wait_recv()

        @pl.when(has_west)
        def _():
            to_east(n).wait_recv()

    load_jac.wait()
    load_perm.wait()
    regimes = jac_s.shape[0]
    for r in range(regimes):
        part = lax.dot_general(perm_s[own_rows, :], jac_s[r], NT, preferred_element_type=F32).astype(BF)
        part = lax.dot_general(part, perm_s[...], NT, preferred_element_type=F32).astype(BF)
        jt_s[r * 2 * width : (r + 1) * 2 * width, :] = part

    swap_misc.wait_recv()
    for i in (0, half_x - 1):
        swap_lam[i].wait_recv()
    for b in range(2):
        cxe_out[b] = misc[b, 0]
    @pl.when(cx_goes)
    def _():
        cx_west.start()

    send_halos(0, a_s)

    lane = iota((width, ny), 1)
    lane1 = iota((nl, ny), 1)

    def north(v):
        inside = (lane if v.shape[0] == width else lane1) < ny - 1
        return jnp.where(inside, pltpu.roll(v, ny - 1, axis=1), 0.0)

    def south(v):
        inside = (lane if v.shape[0] == width else lane1) > 0
        return jnp.where(inside, pltpu.roll(v, 1, axis=1), 0.0)

    def field(v, f):
        return v[f * nl : (f + 1) * nl]

    def to_core(n, x):
        part = col.at[n, x, own_rows, :]
        return remote(part, part, ks.at[n, x], kr.at[n, x], core, t)

    def dyn(n, x, src, dst):
        for b in range(2):
            me = src[x, b]
            cx, cy, hl = misc[b, x], misc[b, half_x + x], misc[b, nx]
            if x == half_x - 1:
                east = e_in[n, b].astype(F32)
                cxe = jnp.where(low, misc[b, nx + 1], cxe_in[b])
            else:
                east, cxe = src[x + 1, b], misc[b, x + 1]
            if x == 0:
                west = w_in[n, b].astype(F32)
                west_u, west_p = west[:nl], west[nl:]
            else:
                west_u, west_p = src[x - 1, b, :nl], src[x - 1, b, 3 * nl : 4 * nl]
            tile = lambda v: jnp.concatenate([v] * nf, axis=0)
            new = me + tile(cxe) * east + north(tile(cy) * me) - tile(cx + cy) * me
            v, p = field(me, 1), field(me, 3)
            d_u = hl * (field(east, 3) - west_p)
            d_v = hl * (north(p) - south(p))
            d_p = hl * (field(east, 0) - west_u + north(v) - south(v))
            zero = jnp.zeros_like(d_u)
            new = new + jnp.concatenate([d_u, d_v, zero, d_p, zero, zero], axis=0)
            dst[x, b] = new
            col[n, x, pl.ds(pl.multiple_of(c * 2 * width + b * width, 16), width), :] = new.astype(BF)
        to_core(n, x).start()

    def phys(n, xs, dst):
        for x in xs:
            to_core(n, x).wait_recv()
        both = jnp.concatenate([col[n, x] for x in xs], axis=1)
        out = jnp.dot(jt_s[...], both, preferred_element_type=F32)
        ops = [jnp.concatenate([op_s[b], op_s[b]], axis=1) for b in range(2)]
        for at, x in enumerate(xs):
            part = out[:, at * ny : (at + 1) * ny]
            reg = reg_ref[pl.ds(n * nx + x0 + x, 1), :]
            sums = g_s[n, slot[x]]
            for b in range(2):
                delta = part[b * width : (b + 1) * width]
                for r in range(1, regimes):
                    row = (2 * r + b) * width
                    delta = jnp.where(reg == r, part[row : row + width], delta)
                forcing = lax.dot_general(ops[b], sums, NT, preferred_element_type=F32)
                dst[x, b] = dst[x, b] + delta.astype(BF).astype(F32) + forcing

    def read_cells():
        all_of(recv_cell.at[pl.ds(0, n_tile - 1), :], ss_cell, rs_cell).wait_recv()
        even = recv_cell[pl.ds(0, n_tile // 2, stride=2), :]
        odd = recv_cell[pl.ds(1, n_tile // 2, stride=2), :]
        key_s[...] = (even + odd).astype(jnp.int32) - 1

    sub16s = iota((16, GROUP * cap), 0).astype(F32)

    def sum_rows(first, last):
        def unpack(g, _):
            s0 = pl.multiple_of(((groups - g + my_group) % groups) * GROUP, GROUP)

            from_group = s0 // GROUP

            @pl.when(from_group != my_group)
            def _():
                all_of(recv_rows.at[pl.ds(0, GROUP)], ss_rows, rs_rows.at[from_group]).wait_recv()

            @pl.when(from_group == my_group)
            def _():
                all_of(recv_rows.at[pl.ds(0, GROUP - 1)], ss_rows, rs_rows.at[from_group]).wait_recv()

            key = jnp.concatenate(
                [key_s[pl.ds(s0 // 2 + q, 1), :] for q in range(GROUP // 2)], axis=1
            )
            at_x = key >> 7
            at_y = (key & 127).astype(F32)
            for x in range(nx):
                kx = jnp.broadcast_to(jnp.where(at_x == x, at_y, -1.0), (16, GROUP * cap)).astype(BF)
                for q in range(ny // 16):
                    hot = kx == (sub16s + 16.0 * q).astype(BF)
                    ohs[x * ny + q * 16 : x * ny + (q + 1) * 16, :] = jnp.where(
                        hot, jnp.ones((), BF), jnp.zeros((), BF)
                    )
            rows = recv_rows[pl.ds(s0, GROUP)].reshape(GROUP * cap, vals)
            acc[...] += jnp.dot(ohs[...], rows, preferred_element_type=F32)
            return 0

        if first == 0:
            acc[...] = jnp.zeros_like(acc)
        lax.fori_loop(first, last, unpack, 0)

    def sums_to_core(k):
        part = g_s.at[mine, pl.ds(2 * k, 2)]
        return remote(part, part, gks.at[k], gkr.at[k], core, t)

    def sums_to_far(k):
        return remote(g_far.at[pl.ds(2 * k, 2)], g_s.at[mine, pl.ds(2 * k, 2)], gzs.at[k], gzr.at[k], far, t)

    def sums_pass_on(k):
        part = g_s.at[far, pl.ds(2 * k, 2)]
        return remote(part, part, gfs.at[k], gfr.at[k], core, t)

    def two_parts(x):
        total = acc[pl.ds(pl.multiple_of(x * ny, ny), ny), :]
        head = total.astype(BF)
        return jnp.concatenate([head, (total - head.astype(F32)).astype(BF)], axis=1)

    def share_sums():
        for k in range(2):
            for i in (2 * k, 2 * k + 1):
                g_far[i] = two_parts(x1 + order[i])
            sums_to_far(k).start()
        for k in range(2):
            for i in (2 * k, 2 * k + 1):
                g_s[mine, i] = two_parts(x0 + order[i])
            sums_to_core(k).start()

    def wait_sums(k, half):
        @pl.when(h != half)
        def _():
            sums_to_far(k).wait_recv()
            sums_pass_on(k).start()

        if half == 0:
            sums_to_core(k).wait_recv()

        @pl.when(h != half)
        def _():
            sums_pass_on(k).wait_recv()

    for i in range(1, half_x - 1):
        swap_lam[i].wait_recv()

    @pl.when(cx_comes)
    def _():
        cx_west.wait_recv()

    for x in inner:
        dyn(0, x, a_s, b_s)
    read_cells()
    sum_rows(0, groups)
    share_sums()
    wait_halos(0)
    for x in outer:
        dyn(0, x, a_s, b_s)
    swap_op.wait_recv()
    now, new = b_s, a_s
    last = a_s if steps % 2 == 0 else b_s

    def keep(x):
        return pltpu.make_async_copy(last.at[x, h], out_hbm.at[x0 + x], ls.at[x])

    def give(at, x):
        return remote(last.at[x, 1 - h], out_hbm.at[at + x], ts.at[x], tr.at[x], far, t)

    def finish(xs):
        for x in xs:
            give(x0, x).start()
            keep(x).start()

    for n in range(steps):
        if n == 0:
            wait_sums(0, 0)
        if n == 2:
            wait_sums(0, 1)
            wait_sums(1, 1)
        phys(n, outer, now)
        if n + 1 < steps:
            send_halos(n + 1, now)
        else:
            finish(outer)
        if n == 0:
            wait_sums(1, 0)
        phys(n, inner, now)
        if n + 1 == steps:
            finish(inner)
            break
        for x in inner:
            dyn(n + 1, x, now, new)
        wait_halos(n + 1)
        for x in outer:
            dyn(n + 1, x, now, new)
        now, new = new, now

    for x in outer + inner:
        keep(x).wait()
        give(x1, x).wait_recv()

    all_of(send_cell.at[0, pl.ds(0, n_tile - 1), :], ss_cell, rs_cell).wait_send()
    all_of(send_rows.at[pl.ds(0, n_tile - 1)], ss_rows, rs_rows.at[0]).wait_send()
    for copy in [swap_misc, swap_op] + swap_lam:
        copy.wait_send()
    for k in range(2):
        sums_to_core(k).wait_send()
        sums_to_far(k).wait_send()
        sums_pass_on(k).wait_send()

    @pl.when(cx_goes)
    def _():
        cx_west.wait_send()

    for i in range(half_x):
        give(x0, i).wait_send()
    for n in range(steps):
        for x in range(half_x):
            to_core(n, x).wait_send()

        @pl.when(has_west)
        def _(n=n):
            to_west(n).wait_send()

        @pl.when(has_east)
        def _(n=n):
            to_east(n).wait_send()


def place_of(levels_all, lev_here, fields):
    core, far, f, l = np.meshgrid(
        np.arange(2), np.arange(2), np.arange(fields), np.arange(lev_here), indexing="ij"
    )
    place = (f * levels_all + (2 * far + core) * lev_here + l).reshape(-1)
    return (place[:, None] == np.arange(place.size)[None, :]).astype(np.float32)


def on_device(
    adjoint_final,
    courant_x,
    courant_y,
    sound,
    phys_jac,
    regime,
    obs_operator,
    obs_rows,
    obs_owner,
    obs_cell,
    obs_count,
):
    fields, nl, nx, ny = adjoint_final.shape
    n_tile = lax.axis_size("tile")
    n_lev = lax.axis_size("lev")
    steps, obs, vals = obs_rows.shape
    cap = max(2, 2 * obs // n_tile)
    regimes = phys_jac.shape[0]
    width = fields * nl
    width_all = width * n_lev
    hx = nx // 2
    perm = jnp.asarray(place_of(nl * n_lev, nl, fields), BF)
    vmem = pl.BlockSpec(memory_space=pltpu.VMEM)
    hbm = pl.BlockSpec(memory_space=pl.ANY)
    V = pltpu.VMEM
    dma = pltpu.SemaphoreType.DMA
    out = pl.pallas_call(
        kernel,
        out_shape=jax.ShapeDtypeStruct((nx, width, ny), F32),
        in_specs=[vmem] * 5 + [pl.BlockSpec(memory_space=pltpu.SMEM)] + [hbm] * 6,
        out_specs=hbm,
        scratch_shapes=[
            V((width * nx, ny), F32),
            V((nl * nx, ny), F32),
            V((nl * nx, ny), F32),
            V((2, obs, vals), BF),
            V((n_tile, cap, vals), BF),
            V((n_tile, cap, vals), BF),
            V((2, n_tile, 128), F32),
            V((n_tile, 128), F32),
            V((n_tile, obs), BF),
            V((2 * cap, obs), BF),
            V((2, 1, obs), F32),
            V((2, 1, obs), jnp.int32),
            V((GROUP * cap, obs), BF),
            V((n_tile // 2, 128), jnp.int32),
            V((nx * ny, GROUP * cap), BF),
            V((nx * ny, vals), F32),
            V((steps, hx, ny, 2 * vals), BF),
            V((hx, ny, 2 * vals), BF),
            V((hx, 2, width, ny), F32),
            V((hx, 2, width, ny), F32),
            V((hx, width, ny), F32),
            V((2, nx + 2, nl, ny), F32),
            V((nx + 2, nl, ny), F32),
            V((2, width, vals), BF),
            V((regimes, width_all, width_all), BF),
            V((width_all, width_all), BF),
            V((regimes * 2 * width, width_all), BF),
            V((steps, hx, width_all, ny), BF),
            V((steps, 2, width, ny), BF),
            V((steps, 2, 2 * nl, ny), BF),
            V((steps, 2, width, ny), BF),
            V((steps, 2, 2 * nl, ny), BF),
            V((2, nl, ny), F32),
            V((2, nl, ny), F32),
            dma((7,)), dma, dma((n_tile // GROUP,)), dma, dma,
            dma((2,)), dma((2,)), dma((2,)), dma((2,)), dma((2,)), dma((2,)),
            dma((hx + 2,)), dma((hx + 2,)), dma((steps,)), dma((steps,)), dma((steps,)), dma((steps,)),
            dma, dma, dma((steps, hx)), dma((steps, hx)), dma((hx,)), dma((hx,)), dma((hx,)),
        ],
        compiler_params=pltpu.CompilerParams(
            collective_id=0, has_side_effects=True, vmem_limit_bytes=56 * 1024 * 1024
        ),
        name="sweep",
    )(
        sound.reshape(1, nl),
        regime.reshape(steps * nx, ny),
        obs_operator.transpose(1, 2, 0).reshape(width, vals),
        obs_owner.reshape(steps, 1, obs),
        obs_cell,
        obs_count.reshape(1, steps),
        adjoint_final.reshape(width * nx, ny),
        courant_x.reshape(nl * nx, ny),
        courant_y.reshape(nl * nx, ny),
        phys_jac,
        perm,
        obs_rows,
    )
    return out.reshape(nx, fields, nl, ny).transpose(1, 2, 0, 3)


def solution(mesh):
    return jax.shard_map(
        on_device,
        mesh=mesh,
        in_specs=(
            P(None, "lev", "tile", None),
            P("lev", "tile", None),
            P("lev", "tile", None),
            P("lev"),
            P(),
            P(None, "tile", None),
            P(None, None, "lev"),
            P(None, "tile", None),
            P(None, "tile", None),
            P(None, "tile"),
            P(None, "tile"),
        ),
        out_specs=P(None, "lev", "tile", None),
        check_vma=False,
    )
```

```python
import jax
import jax.numpy as jnp
import numpy as np
from jax import lax
from jax.experimental import pallas as pl
from jax.experimental.pallas import tpu as pltpu
from jax.sharding import PartitionSpec as P

MESH = pl.DeviceIdType.MESH
BF = jnp.bfloat16
F32 = jnp.float32
NT = (((1,), (1,)), ((), ()))
GROUP = 8


def iota(shape, dim):
    return lax.broadcasted_iota(jnp.int32, shape, dim)


def crosses(t, d, n_tile):
    per_z = n_tile // 4
    apart = jnp.abs(t // per_z - d // per_z)
    odd = (t // GROUP + d // GROUP) % 2 == 1
    return jnp.logical_or(apart == 3, jnp.logical_and(apart == 2, odd))


def kernel(
    sound_ref, reg_ref, op_ref, own_ref, cell_ref, cnt_ref,
    lam_hbm, cx_hbm, cy_hbm, jac_hbm, perm_hbm, rows_hbm, out_hbm,
    lam_ref, cx_ref, cy_ref,
    rows_v, send_rows, recv_rows, send_cell, recv_cell, oh, rc, rank_s, own_s, pmat, key_s, ohs, acc, g_s, g_far,
    a_s, b_s, lam_out, misc, misc_out, op_s, jac_s, perm_s, jt_s, col,
    e_in, w_in, e_out, w_out, cxe_in, cxe_out,
    load_sem, ss_rows, rs_rows, ss_cell, rs_cell, gks, gkr, gzs, gzr, gfs, gfr,
    xs_sem, xr_sem, es, er, ws, wr, cs, cr, ks, kr, ts, tr, ls,
):
    lev = lax.axis_index("lev")
    t = lax.axis_index("tile")
    n_tile, cap, vals = send_rows.shape
    obs = rows_v.shape[1]
    h = lev // 2
    c = lev % 2
    core = lev + 1 - 2 * c
    far = (lev + 2) % 4
    steps, half_x, width_all, ny = col.shape
    nx = 2 * half_x
    width = a_s.shape[2]
    nl = misc.shape[2]
    nf = width // nl
    low = h == t % 2
    x0 = jnp.where(low, 0, half_x)
    x1 = half_x - x0
    groups = n_tile // GROUP
    my_group = t // GROUP
    own_rows = pl.ds(pl.multiple_of(c * 2 * width, 16), 2 * width)

    w_lev, w_tile = jnp.where(low, lev, far), jnp.where(low, t - 1, t)
    e_lev, e_tile = jnp.where(low, far, lev), jnp.where(low, t, t + 1)
    has_west = w_tile >= 0
    has_east = e_tile < n_tile

    def remote(src, dst, ssem, rsem, to_lev, to_tile):
        return pltpu.make_async_remote_copy(
            src_ref=src, dst_ref=dst, send_sem=ssem, recv_sem=rsem,
            device_id={"lev": to_lev, "tile": to_tile}, device_id_type=MESH,
        )

    mine = lev
    sent_steps = (lev, far)
    load_rows = [pltpu.make_async_copy(rows_hbm.at[n], rows_v.at[j], load_sem.at[j]) for j, n in enumerate(sent_steps)]
    load_jac = pltpu.make_async_copy(jac_hbm, jac_s, load_sem.at[2])
    load_perm = pltpu.make_async_copy(perm_hbm, perm_s, load_sem.at[6])
    load_state = [
        pltpu.make_async_copy(src, dst, load_sem.at[3 + i])
        for i, (src, dst) in enumerate(((lam_hbm, lam_ref), (cx_hbm, cx_ref), (cy_hbm, cy_ref)))
    ]
    for load in load_state + load_rows + [load_jac, load_perm]:
        load.start()

    barrier = pltpu.get_barrier_semaphore()

    def greet(i, _):
        d = (t + i) % n_tile
        pl.semaphore_signal(
            barrier, inc=1, device_id={"lev": jnp.where(crosses(t, d, n_tile), far, lev), "tile": d}, device_id_type=MESH
        )
        return 0

    lax.fori_loop(1, n_tile, greet, 0)
    for other in (core, far):
        pl.semaphore_signal(barrier, inc=1, device_id={"lev": other, "tile": t}, device_id_type=MESH)

    def columns(ref, x, rows):
        return ref[pl.ds(x, rows, stride=nx), :]

    same = iota((nl, nl), 0) == iota((nl, nl), 1)
    hs = 0.5 * jnp.sum(jnp.where(same, sound_ref[...], 0.0), axis=1, keepdims=True)
    hs = jnp.broadcast_to(hs, (nl, ny))
    for load in load_state:
        load.wait()
    for i in range(half_x):
        lam_out[i] = columns(lam_ref, x1 + i, width)
        misc_out[i] = columns(cx_ref, x1 + i, nl)
        misc_out[half_x + i] = columns(cy_ref, x1 + i, nl)
        a_s[i, h] = columns(lam_ref, x0 + i, width)
        misc[h, i] = columns(cx_ref, x0 + i, nl)
        misc[h, half_x + i] = columns(cy_ref, x0 + i, nl)
    for ref in (misc_out, misc.at[h]):
        ref[nx] = hs
        ref[nx + 1] = columns(cx_ref, half_x, nl)
    op_s[h] = op_ref[...]

    cx_goes = jnp.logical_and(low, has_west)
    cx_comes = jnp.logical_and(jnp.logical_not(low), has_east)

    @pl.when(jnp.logical_not(cx_comes))
    def _():
        cxe_in[...] = jnp.zeros_like(cxe_in)

    @pl.when(jnp.logical_not(has_west))
    def _():
        w_in[...] = jnp.zeros_like(w_in)

    @pl.when(jnp.logical_not(has_east))
    def _():
        e_in[...] = jnp.zeros_like(e_in)

    upper = jnp.where(iota((128, 256), 0) < iota((128, 256), 1), 1.0, 0.0).astype(BF)
    lane128 = iota((n_tile, 128), 1)

    def rank_rows(j):
        step = sent_steps[j]
        live = iota((1, obs), 1) < cnt_ref[0, step]
        own = jnp.where(live, own_ref[step], -1)
        own_s[j] = own
        oh[...] = jnp.where(own == iota((n_tile, obs), 0), 1.0, 0.0).astype(BF)
        carry = jnp.zeros((n_tile, 128), F32)
        for b in range(obs // 128):
            cols = slice(b * 128, (b + 1) * 128)
            hot = oh[:, cols]
            ex = jnp.dot(hot, upper, preferred_element_type=F32)
            rank_s[j, :, cols] = jnp.sum(hot.astype(F32) * (ex[:, :128] + carry), axis=0, keepdims=True)
            carry = carry + ex[:, 128:]
        rank = jnp.where(live, rank_s[j], -1.0)
        rank_s[j] = rank
        cell = cell_ref[pl.ds(step, 1), :]
        hot = rank == iota((cap, obs), 0).astype(F32)
        rc[:cap] = jnp.where(hot, (cell >> 7).astype(F32), 0.0).astype(BF)
        rc[cap:] = jnp.where(hot, ((cell & 127) + 1).astype(F32), 0.0).astype(BF)
        both = lax.dot_general(oh[...], rc[...], NT, preferred_element_type=F32)
        key = both * 128.0 + pltpu.roll(both, 64, axis=1)
        return jnp.where(lane128 < 64, key, 0.0)

    for j in (0,):
        keys = rank_rows(j)
        send_cell[j] = jnp.where(t % 2 == 0, keys, pltpu.roll(keys, 64, axis=1))

    pl.semaphore_wait(barrier, n_tile + 1)

    inner = list(range(1, half_x - 1))
    outer = [0, half_x - 1]
    order = outer + inner
    slot = {x: i for i, x in enumerate(order)}
    swap_misc = remote(misc_out, misc.at[h], xs_sem.at[half_x], xr_sem.at[half_x], far, t)
    swap_op = remote(op_s.at[h], op_s.at[h], xs_sem.at[half_x + 1], xr_sem.at[half_x + 1], far, t)
    swap_lam = [remote(lam_out.at[i], a_s.at[i, h], xs_sem.at[i], xr_sem.at[i], far, t) for i in range(half_x)]
    swap_misc.start()
    for i in order:
        swap_lam[i].start()
    swap_op.start()

    def cell_copy(d):
        return remote(
            send_cell.at[crosses(t, d, n_tile).astype(jnp.int32), pl.ds(d, 1), :], recv_cell.at[pl.ds(t, 1), :],
            ss_cell, rs_cell, jnp.where(crosses(t, d, n_tile), far, lev), d,
        )

    def row_copy(d):
        return remote(
            send_rows.at[d], recv_rows.at[t], ss_rows, rs_rows.at[my_group],
            jnp.where(crosses(t, d, n_tile), far, lev), d,
        )

    def all_of(buf, ssem, rsem):
        return remote(buf, buf, ssem, rsem, far, t)

    sub16 = iota((16, obs), 0).astype(F32)

    def pack_rows():
        for load in load_rows:
            load.wait()

        def pack(g, _):
            d0 = pl.multiple_of(((3 * g + my_group) % groups) * GROUP, GROUP)
            j = crosses(t, d0, n_tile).astype(jnp.int32)
            for i in range(GROUP):
                key = jnp.where(own_s[j] == d0 + i, rank_s[j], -1.0)
                key = jnp.broadcast_to(key, (16, obs)).astype(BF)
                for q in range(cap // 16):
                    hot = key == (sub16 + 16.0 * q).astype(BF)
                    pmat[i * cap + q * 16 : i * cap + (q + 1) * 16, :] = jnp.where(
                        hot, jnp.ones((), BF), jnp.zeros((), BF)
                    )
            packed = jnp.dot(pmat[...], rows_v[j], preferred_element_type=F32)
            send_rows[pl.ds(d0, GROUP)] = packed.astype(BF).reshape(GROUP, cap, vals)

            def send(i, _):
                d = d0 + i

                @pl.when(d != t)
                def _():
                    row_copy(d).start()

                return 0

            lax.fori_loop(0, GROUP, send, 0)
            return 0

        lax.fori_loop(0, groups, pack, 0)
        recv_rows[t] = send_rows[t]

    for j in (1,):
        keys = rank_rows(j)
        send_cell[j] = jnp.where(t % 2 == 0, keys, pltpu.roll(keys, 64, axis=1))

    def send_cells(i, _):
        cell_copy((t + i) % n_tile).start()
        return 0

    lax.fori_loop(1, n_tile, send_cells, 0)
    recv_cell[pl.ds(t, 1), :] = send_cell[0, pl.ds(t, 1), :]
    pack_rows()

    def to_west(n):
        return remote(e_out.at[n], e_in.at[n], es.at[n], er.at[n], w_lev, w_tile)

    def to_east(n):
        return remote(w_out.at[n], w_in.at[n], ws.at[n], wr.at[n], e_lev, e_tile)

    cx_west = remote(cxe_out, cxe_in, cs, cr, w_lev, w_tile)

    def send_halos(n, src):
        for b in range(2):
            e_out[n, b] = src[0, b].astype(BF)
            last = src[half_x - 1, b]
            w_out[n, b] = jnp.concatenate([last[:nl], last[3 * nl : 4 * nl]], axis=0).astype(BF)

        @pl.when(has_west)
        def _():
            to_west(n).start()

        @pl.when(has_east)
        def _():
            to_east(n).start()

    def wait_halos(n):
        @pl.when(has_east)
        def _():
            to_west(n).wait_recv()

        @pl.when(has_west)
        def _():
            to_east(n).wait_recv()

    load_jac.wait()
    load_perm.wait()
    regimes = jac_s.shape[0]
    for r in range(regimes):
        part = lax.dot_general(perm_s[own_rows, :], jac_s[r], NT, preferred_element_type=F32).astype(BF)
        part = lax.dot_general(part, perm_s[...], NT, preferred_element_type=F32).astype(BF)
        jt_s[r * 2 * width : (r + 1) * 2 * width, :] = part

    swap_misc.wait_recv()
    for i in (0, half_x - 1):
        swap_lam[i].wait_recv()
    for b in range(2):
        cxe_out[b] = misc[b, 0]
    @pl.when(cx_goes)
    def _():
        cx_west.start()

    send_halos(0, a_s)

    lane = iota((width, ny), 1)
    lane1 = iota((nl, ny), 1)

    def north(v):
        inside = (lane if v.shape[0] == width else lane1) < ny - 1
        return jnp.where(inside, pltpu.roll(v, ny - 1, axis=1), 0.0)

    def south(v):
        inside = (lane if v.shape[0] == width else lane1) > 0
        return jnp.where(inside, pltpu.roll(v, 1, axis=1), 0.0)

    def field(v, f):
        return v[f * nl : (f + 1) * nl]

    def to_core(n, x):
        part = col.at[n, x, own_rows, :]
        return remote(part, part, ks.at[n, x], kr.at[n, x], core, t)

    def dyn(n, x, src, dst):
        for b in range(2):
            me = src[x, b]
            cx, cy, hl = misc[b, x], misc[b, half_x + x], misc[b, nx]
            if x == half_x - 1:
                east = e_in[n, b].astype(F32)
                cxe = jnp.where(low, misc[b, nx + 1], cxe_in[b])
            else:
                east, cxe = src[x + 1, b], misc[b, x + 1]
            if x == 0:
                west = w_in[n, b].astype(F32)
                west_u, west_p = west[:nl], west[nl:]
            else:
                west_u, west_p = src[x - 1, b, :nl], src[x - 1, b, 3 * nl : 4 * nl]
            tile = lambda v: jnp.concatenate([v] * nf, axis=0)
            new = me + tile(cxe) * east + north(tile(cy) * me) - tile(cx + cy) * me
            v, p = field(me, 1), field(me, 3)
            d_u = hl * (field(east, 3) - west_p)
            d_v = hl * (north(p) - south(p))
            d_p = hl * (field(east, 0) - west_u + north(v) - south(v))
            zero = jnp.zeros_like(d_u)
            new = new + jnp.concatenate([d_u, d_v, zero, d_p, zero, zero], axis=0)
            dst[x, b] = new
            col[n, x, pl.ds(pl.multiple_of(c * 2 * width + b * width, 16), width), :] = new.astype(BF)
        to_core(n, x).start()

    def phys(n, xs, dst):
        for x in xs:
            to_core(n, x).wait_recv()
        both = jnp.concatenate([col[n, x] for x in xs], axis=1)
        out = jnp.dot(jt_s[...], both, preferred_element_type=F32)
        ops = [jnp.concatenate([op_s[b], op_s[b]], axis=1) for b in range(2)]
        for at, x in enumerate(xs):
            part = out[:, at * ny : (at + 1) * ny]
            reg = reg_ref[pl.ds(n * nx + x0 + x, 1), :]
            sums = g_s[n, slot[x]]
            for b in range(2):
                delta = part[b * width : (b + 1) * width]
                for r in range(1, regimes):
                    row = (2 * r + b) * width
                    delta = jnp.where(reg == r, part[row : row + width], delta)
                forcing = lax.dot_general(ops[b], sums, NT, preferred_element_type=F32)
                dst[x, b] = dst[x, b] + delta.astype(BF).astype(F32) + forcing

    def read_cells():
        all_of(recv_cell.at[pl.ds(0, n_tile - 1), :], ss_cell, rs_cell).wait_recv()
        even = recv_cell[pl.ds(0, n_tile // 2, stride=2), :]
        odd = recv_cell[pl.ds(1, n_tile // 2, stride=2), :]
        key_s[...] = (even + odd).astype(jnp.int32) - 1

    sub16s = iota((16, GROUP * cap), 0).astype(F32)

    def sum_rows(first, last):
        def unpack(g, _):
            s0 = pl.multiple_of(((5 * g + my_group) % groups) * GROUP, GROUP)

            from_group = s0 // GROUP

            @pl.when(from_group != my_group)
            def _():
                all_of(recv_rows.at[pl.ds(0, GROUP)], ss_rows, rs_rows.at[from_group]).wait_recv()

            @pl.when(from_group == my_group)
            def _():
                all_of(recv_rows.at[pl.ds(0, GROUP - 1)], ss_rows, rs_rows.at[from_group]).wait_recv()

            key = jnp.concatenate(
                [key_s[pl.ds(s0 // 2 + q, 1), :] for q in range(GROUP // 2)], axis=1
            )
            at_x = key >> 7
            at_y = (key & 127).astype(F32)
            for x in range(nx):
                kx = jnp.broadcast_to(jnp.where(at_x == x, at_y, -1.0), (16, GROUP * cap)).astype(BF)
                for q in range(ny // 16):
                    hot = kx == (sub16s + 16.0 * q).astype(BF)
                    ohs[x * ny + q * 16 : x * ny + (q + 1) * 16, :] = jnp.where(
                        hot, jnp.ones((), BF), jnp.zeros((), BF)
                    )
            rows = recv_rows[pl.ds(s0, GROUP)].reshape(GROUP * cap, vals)
            acc[...] += jnp.dot(ohs[...], rows, preferred_element_type=F32)
            return 0

        if first == 0:
            acc[...] = jnp.zeros_like(acc)
        lax.fori_loop(first, last, unpack, 0)

    def sums_to_core(k):
        part = g_s.at[mine, pl.ds(2 * k, 2)]
        return remote(part, part, gks.at[k], gkr.at[k], core, t)

    def sums_to_far(k):
        return remote(g_far.at[pl.ds(2 * k, 2)], g_s.at[mine, pl.ds(2 * k, 2)], gzs.at[k], gzr.at[k], far, t)

    def sums_pass_on(k):
        part = g_s.at[far, pl.ds(2 * k, 2)]
        return remote(part, part, gfs.at[k], gfr.at[k], core, t)

    def two_parts(x):
        total = acc[pl.ds(pl.multiple_of(x * ny, ny), ny), :]
        head = total.astype(BF)
        return jnp.concatenate([head, (total - head.astype(F32)).astype(BF)], axis=1)

    def share_sums():
        for k in range(2):
            for i in (2 * k, 2 * k + 1):
                g_far[i] = two_parts(x1 + order[i])
            sums_to_far(k).start()
        for k in range(2):
            for i in (2 * k, 2 * k + 1):
                g_s[mine, i] = two_parts(x0 + order[i])
            sums_to_core(k).start()

    def wait_sums(k, half):
        @pl.when(h != half)
        def _():
            sums_to_far(k).wait_recv()
            sums_pass_on(k).start()

        if half == 0:
            sums_to_core(k).wait_recv()

        @pl.when(h != half)
        def _():
            sums_pass_on(k).wait_recv()

    for i in range(1, half_x - 1):
        swap_lam[i].wait_recv()

    @pl.when(cx_comes)
    def _():
        cx_west.wait_recv()

    for x in inner:
        dyn(0, x, a_s, b_s)
    read_cells()
    sum_rows(0, groups)
    share_sums()
    wait_halos(0)
    for x in outer:
        dyn(0, x, a_s, b_s)
    swap_op.wait_recv()
    now, new = b_s, a_s
    last = a_s if steps % 2 == 0 else b_s

    def keep(x):
        return pltpu.make_async_copy(last.at[x, h], out_hbm.at[x0 + x], ls.at[x])

    def give(at, x):
        return remote(last.at[x, 1 - h], out_hbm.at[at + x], ts.at[x], tr.at[x], far, t)

    def finish(xs):
        for x in xs:
            give(x0, x).start()
            keep(x).start()

    for n in range(steps):
        if n == 0:
            wait_sums(0, 0)
        if n == 2:
            wait_sums(0, 1)
            wait_sums(1, 1)
        phys(n, outer, now)
        if n + 1 < steps:
            send_halos(n + 1, now)
        else:
            finish(outer)
        if n == 0:
            wait_sums(1, 0)
        phys(n, inner, now)
        if n + 1 == steps:
            finish(inner)
            break
        for x in inner:
            dyn(n + 1, x, now, new)
        wait_halos(n + 1)
        for x in outer:
            dyn(n + 1, x, now, new)
        now, new = new, now

    for x in outer + inner:
        keep(x).wait()
        give(x1, x).wait_recv()

    all_of(send_cell.at[0, pl.ds(0, n_tile - 1), :], ss_cell, rs_cell).wait_send()
    all_of(send_rows.at[pl.ds(0, n_tile - 1)], ss_rows, rs_rows.at[0]).wait_send()
    for copy in [swap_misc, swap_op] + swap_lam:
        copy.wait_send()
    for k in range(2):
        sums_to_core(k).wait_send()
        sums_to_far(k).wait_send()
        sums_pass_on(k).wait_send()

    @pl.when(cx_goes)
    def _():
        cx_west.wait_send()

    for i in range(half_x):
        give(x0, i).wait_send()
    for n in range(steps):
        for x in range(half_x):
            to_core(n, x).wait_send()

        @pl.when(has_west)
        def _(n=n):
            to_west(n).wait_send()

        @pl.when(has_east)
        def _(n=n):
            to_east(n).wait_send()


def place_of(levels_all, lev_here, fields):
    core, far, f, l = np.meshgrid(
        np.arange(2), np.arange(2), np.arange(fields), np.arange(lev_here), indexing="ij"
    )
    place = (f * levels_all + (2 * far + core) * lev_here + l).reshape(-1)
    return (place[:, None] == np.arange(place.size)[None, :]).astype(np.float32)


def on_device(
    adjoint_final,
    courant_x,
    courant_y,
    sound,
    phys_jac,
    regime,
    obs_operator,
    obs_rows,
    obs_owner,
    obs_cell,
    obs_count,
):
    fields, nl, nx, ny = adjoint_final.shape
    n_tile = lax.axis_size("tile")
    n_lev = lax.axis_size("lev")
    steps, obs, vals = obs_rows.shape
    cap = max(2, 2 * obs // n_tile)
    regimes = phys_jac.shape[0]
    width = fields * nl
    width_all = width * n_lev
    hx = nx // 2
    perm = jnp.asarray(place_of(nl * n_lev, nl, fields), BF)
    vmem = pl.BlockSpec(memory_space=pltpu.VMEM)
    hbm = pl.BlockSpec(memory_space=pl.ANY)
    V = pltpu.VMEM
    dma = pltpu.SemaphoreType.DMA
    out = pl.pallas_call(
        kernel,
        out_shape=jax.ShapeDtypeStruct((nx, width, ny), F32),
        in_specs=[vmem] * 5 + [pl.BlockSpec(memory_space=pltpu.SMEM)] + [hbm] * 6,
        out_specs=hbm,
        scratch_shapes=[
            V((width * nx, ny), F32),
            V((nl * nx, ny), F32),
            V((nl * nx, ny), F32),
            V((2, obs, vals), BF),
            V((n_tile, cap, vals), BF),
            V((n_tile, cap, vals), BF),
            V((2, n_tile, 128), F32),
            V((n_tile, 128), F32),
            V((n_tile, obs), BF),
            V((2 * cap, obs), BF),
            V((2, 1, obs), F32),
            V((2, 1, obs), jnp.int32),
            V((GROUP * cap, obs), BF),
            V((n_tile // 2, 128), jnp.int32),
            V((nx * ny, GROUP * cap), BF),
            V((nx * ny, vals), F32),
            V((steps, hx, ny, 2 * vals), BF),
            V((hx, ny, 2 * vals), BF),
            V((hx, 2, width, ny), F32),
            V((hx, 2, width, ny), F32),
            V((hx, width, ny), F32),
            V((2, nx + 2, nl, ny), F32),
            V((nx + 2, nl, ny), F32),
            V((2, width, vals), BF),
            V((regimes, width_all, width_all), BF),
            V((width_all, width_all), BF),
            V((regimes * 2 * width, width_all), BF),
            V((steps, hx, width_all, ny), BF),
            V((steps, 2, width, ny), BF),
            V((steps, 2, 2 * nl, ny), BF),
            V((steps, 2, width, ny), BF),
            V((steps, 2, 2 * nl, ny), BF),
            V((2, nl, ny), F32),
            V((2, nl, ny), F32),
            dma((7,)), dma, dma((n_tile // GROUP,)), dma, dma,
            dma((2,)), dma((2,)), dma((2,)), dma((2,)), dma((2,)), dma((2,)),
            dma((hx + 2,)), dma((hx + 2,)), dma((steps,)), dma((steps,)), dma((steps,)), dma((steps,)),
            dma, dma, dma((steps, hx)), dma((steps, hx)), dma((hx,)), dma((hx,)), dma((hx,)),
        ],
        compiler_params=pltpu.CompilerParams(
            collective_id=0, has_side_effects=True, vmem_limit_bytes=56 * 1024 * 1024
        ),
        name="sweep",
    )(
        sound.reshape(1, nl),
        regime.reshape(steps * nx, ny),
        obs_operator.transpose(1, 2, 0).reshape(width, vals),
        obs_owner.reshape(steps, 1, obs),
        obs_cell,
        obs_count.reshape(1, steps),
        adjoint_final.reshape(width * nx, ny),
        courant_x.reshape(nl * nx, ny),
        courant_y.reshape(nl * nx, ny),
        phys_jac,
        perm,
        obs_rows,
    )
    return out.reshape(nx, fields, nl, ny).transpose(1, 2, 0, 3)


def solution(mesh):
    return jax.shard_map(
        on_device,
        mesh=mesh,
        in_specs=(
            P(None, "lev", "tile", None),
            P("lev", "tile", None),
            P("lev", "tile", None),
            P("lev"),
            P(),
            P(None, "tile", None),
            P(None, None, "lev"),
            P(None, "tile", None),
            P(None, "tile", None),
            P(None, "tile"),
            P(None, "tile"),
        ),
        out_specs=P(None, "lev", "tile", None),
        check_vma=False,
    )
```
